128 devices in a mesh: view: 4 (over z), slab: 32 (over y, x, core).
Axes of the slice: x: 4, y: 4, z: 4, core: 2. Of those that a mesh axis runs over, the one named last changes fastest.
Arguments:
- estimate: float32 [1024, 128, 128], P('slab'), may hold values from 0.5 to 2
- recorded: float32 [8, 1024, 128, 128], P('view', 'slab'), may hold values from 0.5 to 2
- psf_taps: float32 [8, 3, 31], P('view'), may hold values from 0.02 to 1
- tile_map: int32 [8, 32, 32], P('view'), may hold values from 0 to 1023, as said below
Outputs:
- new_estimate: float32 [1024, 128, 128], P('slab')
The draws below stay inside these ranges and needn't reach their ends.
Inputs may be any that keep to these rules, and one draw needn't show every extreme that they name: For each view, tile_map[v] is a bijection of the 1024 tiles. Each view slab a takes its 32 tiles from the world slabs thus: 2 tiles from world slab a itself, none from exactly one other, one from each of the rest.
All inputs are finite; a program needn't handle non-finite values.
Results may differ from the reference program's by a relative error of at most 0.0003.
Values sent between devices are 32-bit elements; how exact they have to be, the bound alone decides.
No kernel may reach another device: no remote copies, remote signals or barrier semaphores. Data moves between devices by JAX's collectives and lax.ppermute only.
A program may use at most 128 MiB of HBM per device.

```python
import math
import jax
import jax.numpy as jnp
from jax import lax

TAPS = 31
ZD = 32
YT = 4
NX = 128
GRID = 32
NZ = 1024
NY = 128
VIEWS = 8


def one_view_map(key):
    grid_size = GRID
    keys = jax.random.split(key, 4)
    sigma = jnp.arange(grid_size, dtype=jnp.int32)
    offset = jax.random.randint(keys[1], (), 1, grid_size)
    sigma_other = (jnp.arange(grid_size, dtype=jnp.int32) + offset) % grid_size
    base = jnp.tile(jnp.arange(grid_size, dtype=jnp.int32)[None, :], (grid_size, 1))
    row_lists = jnp.where(base == sigma_other[:, None], sigma[:, None], base)
    row_orders = jax.vmap(lambda sub_key: jax.random.permutation(sub_key, grid_size))(jax.random.split(keys[2], grid_size))
    sources = jnp.take_along_axis(row_lists, row_orders, axis=1).reshape(-1)
    onehot = (sources[:, None] == jnp.arange(grid_size)[None, :]).astype(jnp.int32)
    before = jnp.cumsum(onehot, axis=0) - onehot
    order_rank = jnp.sum(before * onehot, axis=1)
    tile_orders = jax.vmap(lambda sub_key: jax.random.permutation(sub_key, grid_size))(jax.random.split(keys[3], grid_size))
    tiles = tile_orders[sources, order_rank]
    return (sources * grid_size + tiles).reshape(grid_size, grid_size).astype(jnp.int32)


def draw_tile_map(key, part):
    return jax.vmap(one_view_map)(jax.random.split(jax.random.fold_in(key, 17), VIEWS))


def draw_psf_taps(key, part):
    sub_keys = jax.random.split(jax.random.fold_in(key, 29), 3)
    tap_shape = (VIEWS, 3, TAPS)
    wing_taps = jnp.exp(jax.random.uniform(sub_keys[0], tap_shape, jnp.float32, math.log(0.02), math.log(0.1)))
    lobe_taps = jax.random.uniform(sub_keys[1], tap_shape, jnp.float32, 0.5, 1.0)
    lobe_mask = jax.random.bernoulli(sub_keys[2], 0.12, tap_shape)
    centre_tap = lax.broadcasted_iota(jnp.int32, tap_shape, 2) == TAPS // 2
    tap_values = jnp.where(centre_tap, 1.0, jnp.where(lobe_mask, lobe_taps, wing_taps))
    return jnp.clip(tap_values, 0.02, 1.0).astype(jnp.float32)


def levels(own_key, shape, shards, least, top_value):
    factor_of = 1.0
    for axis_at, parts in shards:
        heights = jax.random.uniform(jax.random.fold_in(jax.random.fold_in(own_key, 6), axis_at), (parts,), jnp.float32, least / len(shards), top_value / len(shards))
        factor_of = factor_of * jnp.repeat(jnp.exp(heights), shape[axis_at] // parts).reshape((-1,) + (1,) * (len(shape) - 1 - axis_at))
    return factor_of


def setup_inputs(seed: int = 0) -> dict:
    seeds = jax.random.split(jax.random.key(seed), 5)
    return {
        "estimate": jnp.clip(jnp.exp(math.log(2.0) - 1.3862944 * jax.random.uniform(seeds[0], (NZ, NY, NX), jnp.float32) ** levels(seeds[0], (NZ, NY, NX), ((0, 32),), -0.2, 0.2)), 0.5, 2.0),
        "recorded": jnp.clip(jnp.exp(math.log(2.0) - 1.3862944 * jax.random.uniform(seeds[1], (VIEWS, NZ, NY, NX), jnp.float32) ** levels(seeds[1], (VIEWS, NZ, NY, NX), ((0, 4), (1, 32)), -0.2, 0.2)), 0.5, 2.0),
        "psf_taps": draw_psf_taps(jax.random.fold_in(seeds[4], 71), 0),
        "tile_map": draw_tile_map(jax.random.fold_in(seeds[4], 71), 0),
    }


def blur_axis(volume, weights, axis_number, adjoint):
    moved_volume = jnp.moveaxis(volume, axis_number, 0)
    length = moved_volume.shape[0]
    tap_count = weights.shape[0]
    half_width = tap_count // 2
    padded_ones = jnp.pad(jnp.ones((length,), jnp.float32), half_width)
    divisor = weights[0] * padded_ones[0:length]
    for tap_index in range(1, tap_count):
        divisor = divisor + weights[tap_index] * padded_ones[tap_index:tap_index + length]
    if adjoint:
        moved_volume = moved_volume / divisor[:, None, None]
    padded = jnp.pad(moved_volume, ((half_width, half_width), (0, 0), (0, 0)))
    summed = jnp.zeros_like(moved_volume)
    for tap_index in range(tap_count):
        if adjoint:
            offset = 2 * half_width - tap_index
        else:
            offset = tap_index
        summed = summed + weights[tap_index] * padded[offset:offset + length]
    if not adjoint:
        summed = summed / divisor[:, None, None]
    return jnp.moveaxis(summed, 0, axis_number)


def to_tiles(volume):
    shaped = volume.reshape(GRID, ZD, GRID, YT, NX).transpose(0, 2, 1, 3, 4)
    return shaped.reshape(GRID * GRID, ZD, YT, NX)


def from_tiles(tiles):
    shaped = tiles.reshape(GRID, GRID, ZD, YT, NX).transpose(0, 2, 1, 3, 4)
    return shaped.reshape(NZ, NY, NX)


def reference(estimate, recorded, psf_taps, tile_map):
    world_tiles = to_tiles(estimate)

    def one_view(product, inputs):
        observed, view_taps, view_map = inputs
        weights = view_taps / jnp.sum(view_taps, axis=1, keepdims=True)
        flat_map = view_map.reshape(-1).astype(jnp.int32)
        viewed = from_tiles(world_tiles[flat_map])
        blurred = viewed
        for axis_number in range(3):
            blurred = blur_axis(blurred, weights[axis_number], axis_number, False)
        adjoint_volume = observed / blurred
        for axis_number in range(3):
            adjoint_volume = blur_axis(adjoint_volume, weights[axis_number], axis_number, True)
        placed = jnp.zeros_like(world_tiles).at[flat_map].set(to_tiles(adjoint_volume))
        return product * from_tiles(placed), None

    product, unused = lax.scan(one_view, jnp.ones_like(estimate), (recorded, psf_taps, tile_map))
    return estimate * product
```

```python
import functools

import jax
import jax.numpy as jnp
from jax import lax
from jax.experimental import pallas as pl
from jax.experimental.pallas import tpu as pltpu
from jax.sharding import PartitionSpec as P

TAPS = 31
HALF = 15
ZD = 32
YT = 4
NX = 128
GRID = 32
NY = 128
PAD = 16
NPAD = ZD + 2 * PAD
TILE = YT * ZD
PLANES = 4
CHUNKS = ((0, 2), (2, 4))

F32 = jnp.float32
BF16 = jnp.bfloat16
VMEM = pl.BlockSpec(memory_space=pltpu.VMEM)
SMEM = pl.BlockSpec(memory_space=pltpu.SMEM)


def call(kernel, outs, name, scratch=(), flops=0, moved=0):
    def run(*operands):
        in_specs = [SMEM if jnp.issubdtype(o.dtype, jnp.integer) else VMEM for o in operands]
        return pl.pallas_call(
            kernel,
            out_shape=[jax.ShapeDtypeStruct(s, F32) for s in outs],
            in_specs=in_specs,
            out_specs=[VMEM] * len(outs),
            scratch_shapes=list(scratch),
            name=name,
            cost_estimate=pl.CostEstimate(flops=flops, bytes_accessed=moved, transcendentals=0),
            compiler_params=pltpu.CompilerParams(vmem_limit_bytes=48 << 20),
        )(*operands)

    return run


def halves(x):
    high = x.astype(BF16)
    low = (x - high.astype(F32)).astype(BF16)
    return high, low


def dot(a, b):
    return jnp.dot(a, b, preferred_element_type=F32)


def left_dot(matrix, x):
    high, low = halves(x)
    full = dot(matrix, jnp.concatenate([high, low], axis=0))
    rows = full.shape[0] // 2
    return full[:rows] + full[rows:]


def right_dot(x, matrix):
    high, low = halves(x)
    full = dot(jnp.concatenate([high, low], axis=1), matrix)
    return full[:, :NX] + full[:, NX:]


def pack_kernel(table, est, send, kept):
    def move(tile, ref, slot):
        for j in range(YT):
            ref[slot, pl.ds(j * ZD, ZD), :] = est[pl.ds(tile * YT + j, ZD, stride=NY), :]

    def step(slot, carry):
        move(table[slot], send, slot)
        return carry

    lax.fori_loop(0, GRID, step, 0)
    move(table[GRID], kept, 0)


def unpack_kernel(table, recv, kept, low, high):
    def put(source, c):
        for j in range(YT):
            at = pl.multiple_of((c * YT + j) * PAD, PAD)
            low[pl.ds(at, PAD), :] = source[pl.ds(j * ZD, PAD), :]
            high[pl.ds(at, PAD), :] = source[pl.ds(j * ZD + PAD, PAD), :]

    def step(c, carry):
        slot = table[c]

        @pl.when(slot < GRID)
        def _():
            put(recv.at[slot], c)

        @pl.when(slot == GRID)
        def _():
            put(kept.at[0], c)

        return carry

    lax.fori_loop(0, GRID, step, 0)


def padded_pair(parts, first, second):
    columns = []
    for y in (first, second):
        at = pl.multiple_of(y * PAD, PAD)
        columns.append(jnp.concatenate([p[pl.ds(at, PAD), :] for p in parts], axis=0))
    return jnp.concatenate(columns, axis=1)


def blur_kernel(top, low, high, bottom, rec, zmat, xmat, ymat, ymat_t, xmat_t, out_low, out_high, work):
    parts = (top, low, high, bottom)

    def forward(group, carry):
        rows = []
        for pair in range(2):
            y = group * 4 + pair * 2
            blurred = left_dot(zmat[...], padded_pair(parts, y, y + 1))
            rows += [blurred[:, :NX], blurred[:, NX:]]
        done = right_dot(jnp.concatenate(rows, axis=0), xmat[...])
        work[pl.ds(pl.multiple_of(group * 4 * ZD, 4 * ZD), 4 * ZD), :] = done
        return carry

    lax.fori_loop(0, NY // 4, forward, 0)

    for base, out in ((0, out_low), (PAD, out_high)):

        def backward(step, carry, base=base, out=out):
            zz = step * 2
            z = base + zz
            x = jnp.concatenate([work[pl.ds(z + i, NY, stride=ZD), :] for i in range(2)], axis=1)
            seen = jnp.concatenate(
                [rec[pl.ds(pl.multiple_of((z + i) * NY, NY), NY), :] for i in range(2)], axis=1
            )
            ratio = seen / left_dot(ymat[...], x)
            back = left_dot(ymat_t[...], ratio)
            back = right_dot(jnp.concatenate([back[:, :NX], back[:, NX:]], axis=0), xmat_t[...])
            for i in range(2):
                out[pl.ds(zz + i, NY, stride=PAD), :] = back[i * NY : (i + 1) * NY]
            return carry

        lax.fori_loop(0, PAD // 2, backward, 0)


def adjoint_kernel(first, last, table, top, low, high, bottom, zmat, send, kept):
    parts = (top, low, high, bottom)

    def move(c, ref, slot):
        for j in range(first, last, 2):
            y = c * YT + j
            done = left_dot(zmat[...], padded_pair(parts, y, y + 1))
            at = (j - first) * ZD
            ref[slot, pl.ds(at, ZD), :] = done[:, :NX]
            ref[slot, pl.ds(at + ZD, ZD), :] = done[:, NX:]

    def step(slot, carry):
        move(table[slot], send, slot)
        return carry

    lax.fori_loop(0, GRID, step, 0)
    move(table[GRID], kept, 0)


def product_kernel(table0, table1, recv0, recv1, kept0, kept1, out):
    def step(t, carry):
        s0 = table0[t]
        s1 = table1[t]
        out[t] = recv0[jnp.minimum(s0, GRID - 1)] * recv1[jnp.minimum(s1, GRID - 1)]

        @pl.when((s0 == GRID) & (s1 < GRID))
        def _():
            out[t] = kept0[0] * recv1[s1]

        @pl.when((s1 == GRID) & (s0 < GRID))
        def _():
            out[t] = recv0[s0] * kept1[0]

        @pl.when((s1 == GRID) & (s0 == GRID))
        def _():
            out[t] = kept0[0] * kept1[0]

        return carry

    lax.fori_loop(0, GRID, step, 0)


def quarter_kernel(arrived, out):
    out[...] = (arrived[0] * arrived[1]) * (arrived[2] * arrived[3])


def final_kernel(place, est, *refs):
    out = refs[-1]
    pieces = refs[:-1]
    quarter = GRID // PLANES
    for chunk, (first, last) in enumerate(CHUNKS):
        for hop in range(PLANES):
            piece = pieces[chunk * PLANES + hop]
            base = place[hop] * quarter

            def step(t, carry, piece=piece, base=base, first=first, last=last):
                for j in range(first, last):
                    rows = pl.ds((base + t) * YT + j, ZD, stride=NY)
                    out[rows, :] = est[rows, :] * piece[t, pl.ds((j - first) * ZD, ZD), :]
                return carry

            lax.fori_loop(0, quarter, step, 0)


def stacked(matrix, axis):
    high = lax.reduce_precision(matrix, 8, 7)
    low = matrix - high
    if axis == 0:
        both = jnp.concatenate([high, low], axis=-2)
        return jnp.concatenate([both, both], axis=-1).astype(BF16)
    both = jnp.concatenate([high, low], axis=-1)
    return jnp.concatenate([both, both], axis=-2).astype(BF16)


def band(weights, positions):
    taps = jnp.arange(TAPS, dtype=jnp.int32)[None, :, None, None]
    return jnp.sum(jnp.where(positions[None, None] == taps, weights[:, :, None, None], 0.0), axis=1)


def bands(psf_taps, own):
    weights = psf_taps / jnp.sum(psf_taps, axis=-1, keepdims=True)
    i = jnp.arange(NX, dtype=jnp.int32)
    plain = band(weights[:, 1:].reshape(-1, TAPS), i[:, None] - i[None, :] + HALF)
    plain = plain / jnp.sum(plain, axis=1, keepdims=True)
    plain = plain.reshape(-1, 2, NX, NX)
    turned = plain.transpose(0, 1, 3, 2)
    ymat, xmat = turned[:, 0], plain[:, 1]
    ymat_t, xmat_t = plain[:, 0], turned[:, 1]

    wz = weights[:, 0]
    rows = own * ZD + jnp.arange(NPAD, dtype=jnp.int32) - PAD
    reach = rows[None, :] + jnp.arange(TAPS, dtype=jnp.int32)[:, None] - HALF
    inside = (reach >= 0) & (reach < GRID * ZD)
    divisor = jnp.sum(jnp.where(inside[None], wz[:, :, None], 0.0), axis=1)
    divisor = jnp.where((rows >= 0) & (rows < GRID * ZD), divisor, 1.0)
    k = jnp.arange(NPAD, dtype=jnp.int32)[None, :]
    o = jnp.arange(ZD, dtype=jnp.int32)[:, None]
    zmat = band(wz, k - o - 1) / divisor[:, PAD : PAD + ZD, None]
    zmat_t = band(wz, o - k + 2 * PAD - 1) / divisor[:, None, :]
    return (
        stacked(zmat, 0),
        stacked(xmat, 1),
        stacked(ymat, 0),
        stacked(ymat_t, 0),
        stacked(xmat_t, 1),
        stacked(zmat_t, 0),
    )


def tables(tile_map, own):
    source = tile_map // GRID
    tile = tile_map % GRID
    c = jnp.arange(GRID, dtype=jnp.int32)
    slots = jnp.arange(GRID + 1, dtype=jnp.int32)
    own_source = lax.dynamic_index_in_dim(source, own, 1, keepdims=False)
    own_tile = lax.dynamic_index_in_dim(tile, own, 1, keepdims=False)
    mine = own_source == own
    earlier = mine[:, None, :] & (c[None, :] < c[:, None])[None]
    second = mine & jnp.any(earlier, axis=2)
    second_at = second[:, None, :] & (c == own)[None, :, None]
    outgoing = (source == own) & ~second_at
    pack = jnp.sum(jnp.where(outgoing, tile, 0), axis=2)
    last = jnp.sum(jnp.where(second, own_tile, 0), axis=1, keepdims=True)
    pack = jnp.concatenate([pack, last], axis=1)
    place = jnp.where(second, GRID, own_source)
    chosen = jnp.sum(jnp.where(place[:, None, :] == slots[None, :, None], c[None, None, :], 0), axis=2)
    value = jnp.where(second_at, GRID, c[None, :, None])
    wanted = (own * GRID + c)[None, :, None, None] == tile_map[:, None]
    arriving = jnp.sum(jnp.where(wanted, value[:, None], 0), axis=(2, 3))
    return pack, place, chosen, arriving


def shifted(value, axis, hop, ring):
    count = lax.axis_size(axis)
    pairs = [(i, (i + hop) % count) for i in range(count) if ring or 0 <= i + hop < count]
    return lax.ppermute(value, axis, pairs)


def local(estimate, recorded, psf_taps, tile_map):
    own = lax.axis_index("slab")
    plane = lax.axis_index("view")
    pack, place, chosen, arriving = tables(tile_map, own)
    mats = bands(psf_taps, own)
    est = estimate.reshape(ZD * NY, NX)
    rec = recorded.reshape(-1, ZD * NY, NX)
    views = rec.shape[0]
    buffer = (GRID, TILE, NX)
    strip = (NY * PAD, NX)
    big = TILE * NX * 4 * GRID

    sent = [
        call(pack_kernel, (buffer, (1, TILE, NX)), "pack", moved=2 * big)(pack[v], est)
        for v in range(views)
    ]
    returned = [[] for _ in CHUNKS]
    for v in range(views):
        send, kept = sent[v]
        recv = lax.all_to_all(send, "slab", 0, 0, tiled=True)
        low, high = call(unpack_kernel, (strip, strip), "unpack", moved=2 * big)(place[v], recv, kept)
        top = shifted(high, "slab", 1, False)
        bottom = shifted(low, "slab", -1, False)
        low, high = call(
            blur_kernel,
            (strip, strip),
            "blur",
            scratch=[pltpu.VMEM((NY * ZD, NX), F32)],
            flops=10 << 30,
            moved=4 * big,
        )(top, low, high, bottom, rec[v], *[m[v] for m in mats[:5]])
        top = shifted(high, "slab", 1, False)
        bottom = shifted(low, "slab", -1, False)
        for n, (first, last) in enumerate(CHUNKS):
            rows = (last - first) * ZD
            send, kept = call(
                functools.partial(adjoint_kernel, first, last),
                ((GRID, rows, NX), (1, rows, NX)),
                "adjoint",
                flops=1 << 30,
                moved=2 * big,
            )(chosen[v], top, low, high, bottom, mats[5][v])
            returned[n].append((send, kept))
    pieces = []
    for n, (first, last) in enumerate(CHUNKS):
        rows = (last - first) * ZD
        back = [lax.all_to_all(send, "slab", 0, 0, tiled=True) for send, _ in returned[n]]
        (product,) = call(product_kernel, ((GRID, rows, NX),), "product", moved=2 * big)(
            arriving[0], arriving[1], *back, *[kept for _, kept in returned[n]]
        )
        spread = lax.all_to_all(product, "view", 0, 0, tiled=True)
        quarter = GRID // PLANES
        (mine,) = call(quarter_kernel, ((quarter, rows, NX),), "quarter", moved=big)(
            spread.reshape(PLANES, quarter, rows, NX)
        )
        pieces += [mine] + [shifted(mine, "view", hop, True) for hop in range(1, PLANES)]
    where = (plane - jnp.arange(PLANES, dtype=jnp.int32)) % PLANES
    (out,) = call(final_kernel, ((ZD * NY, NX),), "final", moved=3 * big)(where, est, *pieces)
    return out.reshape(estimate.shape)


def solution(mesh):
    in_specs = (
        P("slab", None, None),
        P("view", "slab", None, None),
        P("view", None, None),
        P("view", None, None),
    )
    out_specs = P("slab", None, None)
    return jax.shard_map(local, mesh=mesh, in_specs=in_specs, out_specs=out_specs, check_vma=False)
```

```python
import functools

import jax
import jax.numpy as jnp
from jax import lax
from jax.experimental import pallas as pl
from jax.experimental.pallas import tpu as pltpu
from jax.sharding import PartitionSpec as P


TAPS = 31
HALF = 15
ZD = 32
YT = 4
NX = 128
GRID = 32
NY = 128
PAD = 16
NPAD = ZD + 2 * PAD
PLANES = 4
STEPS = 4
ROWS = ZD // STEPS
PITCH = NY + 8
WORK = ZD + 8

F32 = jnp.float32
BF16 = jnp.bfloat16
VMEM = pl.BlockSpec(memory_space=pltpu.VMEM)
SMEM = pl.BlockSpec(memory_space=pltpu.SMEM)
ANY = pl.BlockSpec(memory_space=pl.ANY)


def call(kernel, operands, outs, ins=None, out_specs=None, grid=(), scratch=(), flops=0, moved=0, far=(), alias=None):
    ins = ins or {}
    in_specs = [
        ins.get(n, SMEM if jnp.issubdtype(o.dtype, jnp.integer) else VMEM) for n, o in enumerate(operands)
    ]
    return pl.pallas_call(
        kernel,
        out_shape=[pltpu.HBM(s, F32) if n in far else jax.ShapeDtypeStruct(s, F32) for n, s in enumerate(outs)],
        grid=grid,
        in_specs=in_specs,
        out_specs=out_specs or [VMEM] * len(outs),
        scratch_shapes=list(scratch),
        input_output_aliases=alias or {},
        cost_estimate=pl.CostEstimate(flops=flops, bytes_accessed=moved, transcendentals=0),
        compiler_params=pltpu.CompilerParams(vmem_limit_bytes=24 << 20),
    )(*operands)


def halves(x):
    high = x.astype(BF16)
    low = (x - high.astype(F32)).astype(BF16)
    return high, low


def dot(a, b):
    return jnp.dot(a, b, preferred_element_type=F32)


def left_dot(matrix, x):
    high, low = halves(x)
    full = dot(matrix, jnp.concatenate([high, low], axis=0))
    rows = full.shape[0] // 2
    return full[:rows] + full[rows:]


def right_dot(x, matrix):
    high, low = halves(x)
    full = dot(jnp.concatenate([high, low], axis=1), matrix)
    return full[:, :NX] + full[:, NX:]


def pack_kernel(table, last, est, send, kept0, kept1, turned):
    for z in range(ROWS):
        turned[pl.ds(z * PITCH, NY), :] = est[pl.ds(z * NY, NY), :]

    def rows(tile, j):
        return turned[pl.ds(tile * YT + j, ROWS, stride=PITCH), :]

    def step(slot, carry):
        for v in range(2):
            tile = table[v, slot]
            for j in range(YT):
                send[slot, v, j] = rows(tile, j)
        return carry

    lax.fori_loop(0, GRID, step, 0, unroll=4)
    for v, kept in enumerate((kept0, kept1)):
        for j in range(YT):
            kept[0, j] = rows(last[v], j)


def unpack_kernel(v, table, recv, kept, low, high, sems):
    def put(source, c):
        at = pl.ds(pl.multiple_of(c * YT, YT), YT)
        pltpu.make_async_copy(source.at[:, pl.ds(0, PAD), :], low.at[at], sems.at[0]).start()
        pltpu.make_async_copy(source.at[:, pl.ds(PAD, PAD), :], high.at[at], sems.at[1]).start()

    def step(c, carry):
        slot = table[v, c]

        @pl.when(slot < GRID)
        def _():
            put(recv.at[slot, v], c)

        @pl.when(slot == GRID)
        def _():
            put(kept.at[0], c)

        return carry

    lax.fori_loop(0, GRID, step, 0)
    pltpu.make_async_copy(low, low, sems.at[0]).wait()
    pltpu.make_async_copy(high, high, sems.at[1]).wait()


def padded_pair(parts, *pair):
    columns = [jnp.concatenate([p[y] for p in parts], axis=0) for y in pair]
    return jnp.concatenate(columns, axis=1)


def blur_kernel(v, top, low, high, bottom, rec, zmat, xmat, ymat, ymat_t, xmat_t, out_low, out_high, work, seen_rows, sem):
    zmat, xmat, ymat, ymat_t, xmat_t = (r.at[0] for r in (zmat, xmat, ymat, ymat_t, xmat_t))
    parts = (top, low, high, bottom)
    fetch = pltpu.make_async_copy(rec.at[v], seen_rows, sem)
    fetch.start()

    def forward(group, carry):
        rows = []
        for pair in range(2):
            y = group * 4 + pair * 2
            blurred = left_dot(zmat[...], padded_pair(parts, y, y + 1))
            rows += [blurred[:, :NX], blurred[:, NX:]]
        done = right_dot(jnp.concatenate(rows, axis=0), xmat[...])
        for i in range(4):
            at = pl.multiple_of((group * 4 + i) * WORK, 8)
            work[pl.ds(at, ZD), :] = done[i * ZD : (i + 1) * ZD]
        return carry

    lax.fori_loop(0, NY // 4, forward, 0, unroll=8)
    fetch.wait()

    for base, out in ((0, out_low), (PAD, out_high)):

        def backward(step, carry, base=base, out=out):
            zz = step * 2
            z = base + zz
            x = jnp.concatenate([work[pl.ds(z + i, NY, stride=WORK), :] for i in range(2)], axis=1)
            seen = jnp.concatenate(
                [seen_rows[pl.ds(pl.multiple_of((z + i) * NY, NY), NY), :] for i in range(2)], axis=1
            )
            ratio = seen / left_dot(ymat[...], x)
            back = left_dot(ymat_t[...], ratio)
            back = right_dot(jnp.concatenate([back[:, :NX], back[:, NX:]], axis=0), xmat_t[...])
            for i in range(2):
                out[pl.ds(zz + i, NY, stride=PAD), :] = back[i * NY : (i + 1) * NY]
            return carry

        lax.fori_loop(0, PAD // 2, backward, 0, unroll=8)


def adjoint_first_kernel(v, table, top, low, high, bottom, zmat, *refs):
    parts = (top, low, high, bottom)
    send, kept = refs[-2:]
    slots = send.shape[0]
    base = pl.program_id(0) * slots

    def move(c):
        done = left_dot(zmat[v], padded_pair(parts, c * YT, c * YT + 1))
        return done[:, :NX], done[:, NX:]

    def step(slot, carry):
        send[slot, 0, 0], send[slot, 0, 1] = move(table[v, base + slot])
        return carry

    lax.fori_loop(0, slots, step, 0, unroll=slots)

    @pl.when(pl.program_id(0) == 0)
    def _():
        kept[0], kept[1] = move(table[v, GRID])


def adjoint_last_kernel(v, table, plane, top, low, high, bottom, zmat, *refs):
    parts = (top, low, high, bottom)
    *outs, work = refs

    def step(slot, carry):
        y = table[v, slot] * YT + 2
        done = left_dot(zmat[v], padded_pair(parts, y, y + 1))
        work[slot, pl.ds(0, ZD), :] = done[:, :NX]
        work[slot, pl.ds(ZD, ZD), :] = done[:, NX:]
        return carry

    lax.fori_loop(0, GRID + 1, step, 0, unroll=11)
    for hop, out in enumerate(outs):
        quarter = lax.rem(plane[0] + hop, PLANES)
        out[...] = work[:, pl.ds(pl.multiple_of(quarter * PAD, PAD), PAD), :]


def gather_kernel(*refs):
    *parts, send, kept, sems = refs
    copies = []
    for n, part in enumerate(parts):
        at = (n // 2, n % 2)
        copies.append(pltpu.make_async_copy(part.at[pl.ds(0, GRID)], send.at[:, at[0], at[1]], sems.at[n]))
        copies[-1].start()
    for n, part in enumerate(parts):
        kept[n // 2, n % 2] = part[GRID]
    for copy in copies:
        copy.wait()


def product_first_kernel(table, plane, recv, kept0, kept1, *outs):
    quarter = GRID // PLANES
    for hop, out in enumerate(outs):
        base = lax.rem(plane[0] + hop, PLANES) * quarter

        def step(n, carry, out=out, base=base):
            factors = []
            for v, kept in enumerate((kept0, kept1)):
                slot = table[v, base + n]
                factors.append(jnp.where(slot == GRID, kept[...], recv[jnp.minimum(slot, GRID - 1), v]))
            out[n] = factors[0] * factors[1]
            return carry

        lax.fori_loop(0, quarter, step, 0, unroll=2)


def product_last_kernel(*refs):
    *tables, recv, kept, out = refs

    def step(t, carry):
        factors = []
        for n, table in enumerate(tables):
            for v in range(2):
                slot = table[v, t]
                factors.append(jnp.where(slot == GRID, kept[n, v], recv[jnp.minimum(slot, GRID - 1), n, v]))
        while len(factors) > 1:
            factors = [a * b for a, b in zip(factors[::2], factors[1::2])]
        out[t] = factors[0]
        return carry

    lax.fori_loop(0, GRID, step, 0, unroll=4)


def quarter_kernel(first, second, third, fourth, out):
    out[...] = (first[...] * second[...]) * (third[...] * fourth[...])


def final_kernel(place, est, *refs):
    *pieces, out, turned = refs
    quarter = GRID // PLANES
    at = pl.program_id(0)
    for hop in range(PLANES):
        piece = pieces[hop]
        base = place[hop] * quarter
        for t in range(quarter):
            for j in range(2):
                turned[pl.ds((base + t) * YT + j, ROWS, stride=PITCH), :] = piece[t, j]
    for hop in range(PLANES):
        piece = pieces[PLANES + hop]
        own = place[hop]

        @pl.when(own % 2 == at // 2)
        def _(piece=piece, own=own):
            rows = pl.ds(pl.multiple_of((at % 2) * ROWS, ROWS), ROWS)
            for t in range(GRID):
                turned[pl.ds(t * YT + 2 + own // 2, ROWS, stride=PITCH), :] = piece[t, rows]

    for z in range(ROWS):
        rows = pl.ds(z * NY, NY)
        out[rows, :] = est[rows, :] * turned[pl.ds(z * PITCH, NY), :]


def stacked(matrix, axis):
    high = lax.reduce_precision(matrix, 8, 7)
    low = matrix - high
    if axis == 0:
        both = jnp.concatenate([high, low], axis=-2)
        return jnp.concatenate([both, both], axis=-1).astype(BF16)
    both = jnp.concatenate([high, low], axis=-1)
    return jnp.concatenate([both, both], axis=-2).astype(BF16)


def band(weights, positions):
    taps = jnp.arange(TAPS, dtype=jnp.int32)[None, :, None, None]
    return jnp.sum(jnp.where(positions[None, None] == taps, weights[:, :, None, None], 0.0), axis=1)


def bands(psf_taps, own):
    weights = psf_taps / jnp.sum(psf_taps, axis=-1, keepdims=True)
    i = jnp.arange(NX, dtype=jnp.int32)
    plain = band(weights[:, 1:].reshape(-1, TAPS), i[:, None] - i[None, :] + HALF)
    plain = plain / jnp.sum(plain, axis=1, keepdims=True)
    plain = plain.reshape(-1, 2, NX, NX)
    turned = plain.transpose(0, 1, 3, 2)
    ymat, xmat = turned[:, 0], plain[:, 1]
    ymat_t, xmat_t = plain[:, 0], turned[:, 1]

    wz = weights[:, 0]
    rows = own * ZD + jnp.arange(NPAD, dtype=jnp.int32) - PAD
    reach = rows[None, :] + jnp.arange(TAPS, dtype=jnp.int32)[:, None] - HALF
    inside = (reach >= 0) & (reach < GRID * ZD)
    divisor = jnp.sum(jnp.where(inside[None], wz[:, :, None], 0.0), axis=1)
    divisor = jnp.where((rows >= 0) & (rows < GRID * ZD), divisor, 1.0)
    k = jnp.arange(NPAD, dtype=jnp.int32)[None, :]
    o = jnp.arange(ZD, dtype=jnp.int32)[:, None]
    zmat = band(wz, k - o - 1) / divisor[:, PAD : PAD + ZD, None]
    zmat_t = band(wz, o - k + 2 * PAD - 1) / divisor[:, None, :]
    return (
        stacked(zmat, 0),
        stacked(xmat, 1),
        stacked(ymat, 0),
        stacked(ymat_t, 0),
        stacked(xmat_t, 1),
        stacked(zmat_t, 0),
    )


def tables(tile_map, own):
    source = tile_map // GRID
    tile = tile_map % GRID
    c = jnp.arange(GRID, dtype=jnp.int32)
    slots = jnp.arange(GRID + 1, dtype=jnp.int32)
    key = c[None, None, :] * GRID + tile
    outgoing = source == own
    pack = jnp.min(jnp.where(outgoing, key, GRID * GRID - 1), axis=2) % GRID
    inner = outgoing & (c == own)[None, :, None]
    last_key = jnp.max(jnp.where(inner, key, 0), axis=(1, 2))
    last = last_key % GRID
    own_source = lax.dynamic_index_in_dim(source, own, 1, keepdims=False)
    second = c[None, :] == (last_key // GRID)[:, None]
    place = jnp.where(second, GRID, own_source)
    chosen = jnp.sum(jnp.where(place[:, None, :] == slots[None, :, None], c[None, None, :], 0), axis=2)
    second_at = second[:, None, :] & (c == own)[None, :, None]
    value = jnp.where(second_at, GRID, c[None, :, None])
    wanted = (own * GRID + c)[None, :, None, None] == tile_map[:, None]
    arriving = jnp.sum(jnp.where(wanted, value[:, None], 0), axis=(2, 3))
    return pack, last, place, chosen, arriving


def shifted(value, axis, hop, ring):
    count = lax.axis_size(axis)
    pairs = [(i, (i + hop) % count) for i in range(count) if ring or 0 <= i + hop < count]
    return lax.ppermute(value, axis, pairs)


def exchange(value, axis):
    return lax.all_to_all(value, axis, 0, 0, tiled=True)


def after(value, *others):
    return lax.optimization_barrier((value, *others))[0]


def local(estimate, recorded, psf_taps, tile_map):
    own = lax.axis_index("slab")
    plane = lax.axis_index("view")
    pack, last, place, chosen, arriving = tables(tile_map, own)
    mats = bands(psf_taps, own)
    est = estimate.reshape(ZD * NY, NX)
    far_est = pltpu.with_memory_space_constraint(est, pltpu.HBM)
    rec = recorded.reshape(-1, ZD * NY, NX)
    strip = (NY, PAD, NX)
    big = ZD * NY * NX * 4

    def unpacked(v, recv, kept):
        return call(
            functools.partial(unpack_kernel, v),
            (place, recv, kept),
            (strip, strip),
            ins={1: ANY, 2: ANY},
            scratch=[pltpu.SemaphoreType.DMA((2,))],
            moved=2 * big,
        )

    def padded(low, high):
        return shifted(high, "slab", 1, False), low, high, shifted(low, "slab", -1, False)

    def blurred(v, parts):
        low, high = call(
            functools.partial(blur_kernel, v),
            (*parts, far_rec, *mats[:5]),
            ((NY * PAD, NX), (NY * PAD, NX)),
            ins={4: ANY}
            | {5 + n: pl.BlockSpec((1, *m.shape[1:]), lambda s: (v, 0, 0)) for n, m in enumerate(mats[:5])},
            grid=(1,),
            scratch=[
                pltpu.VMEM((NY * WORK, NX), F32),
                pltpu.VMEM((ZD * NY, NX), F32),
                pltpu.SemaphoreType.DMA,
            ],
            flops=5 << 30,
            moved=4 * big,
        )
        return low.reshape(strip), high.reshape(strip)

    far_rec = pltpu.with_memory_space_constraint(rec, pltpu.HBM)
    views = rec.shape[0]
    steps = lambda *block: pl.BlockSpec(block, lambda s: (*[0] * (len(block) - 2), s, 0))
    send, *kept = call(
        pack_kernel,
        (pack, last, far_est),
        ((GRID, views, YT, ZD, NX), (1, YT, ZD, NX), (1, YT, ZD, NX)),
        ins={2: steps(ROWS * NY, NX)},
        out_specs=[
            steps(GRID, views, YT, ROWS, NX),
            steps(1, YT, ROWS, NX),
            steps(1, YT, ROWS, NX),
        ],
        grid=(STEPS,),
        scratch=[pltpu.VMEM((ROWS * PITCH, NX), F32)],
        moved=2 * big,
        far=(0, 1, 2),
    )
    recv = exchange(send, "slab")
    places = [arriving] + [shifted(arriving, "view", hop, True) for hop in range(1, PLANES)]
    recv, *rest = lax.optimization_barrier((recv, *mats, *places))
    mats, places = rest[: len(mats)], rest[len(mats) :]
    parts0 = padded(*unpacked(0, recv, kept[0]))
    recv = after(recv, parts0[1])
    parts1 = padded(*unpacked(1, recv, kept[1]))
    back0 = blurred(0, parts0)
    ready0 = padded(*back0)
    parts1 = lax.optimization_barrier((*parts1, *back0))[:4]
    back1 = blurred(1, parts1)
    ready1 = padded(*back1)
    half = (GRID, views, 2, ZD, NX)

    def adjoint_first(v, parts, buffer=None):
        operands = (chosen, *parts, mats[5])
        return call(
            functools.partial(adjoint_first_kernel, v),
            operands if buffer is None else (*operands, buffer),
            (half, (2, ZD, NX)),
            ins={6: ANY},
            out_specs=[
                pl.BlockSpec((GRID // STEPS, 1, 2, ZD, NX), lambda s: (s, v, 0, 0, 0)),
                pl.BlockSpec((2, ZD, NX), lambda s: (0, 0, 0)),
            ],
            grid=(STEPS,),
            flops=1 << 30,
            moved=2 * big,
            far=(0,),
            alias={} if buffer is None else {6: 0},
        )

    def adjoint_last(v, parts):
        return call(
            functools.partial(adjoint_last_kernel, v),
            (chosen, plane.reshape(1), *parts, mats[5]),
            ((GRID + 1, PAD, NX),) * PLANES,
            scratch=[pltpu.VMEM((GRID + 1, 2 * ZD, NX), F32)],
            flops=1 << 30,
            moved=2 * big,
        )

    def across(parts):
        return [shifted(p, "view", hop, True) for hop, p in enumerate(parts) if hop]

    last0 = adjoint_last(0, ready0)
    last0 = [last0[0], *across(last0)]
    send, kept0 = adjoint_first(0, ready0)
    send, kept1 = adjoint_first(1, ready1, send)
    recv = exchange(send, "slab")
    last1 = adjoint_last(1, ready1)
    last1 = [last1[0], *across(last1)]
    send, kept = call(
        gather_kernel,
        [part for pair in zip(last0, last1) for part in pair],
        ((GRID, PLANES, views, PAD, NX), (PLANES, views, PAD, NX)),
        out_specs=[ANY, VMEM],
        scratch=[pltpu.SemaphoreType.DMA((PLANES * views,))],
        moved=2 * big,
        far=(0,),
    )
    recv1 = exchange(after(send, recv), "slab")
    block = (GRID // PLANES, 2, ZD, NX)
    products = call(
        product_first_kernel, (arriving, plane.reshape(1), recv, kept0, kept1), (block,) * PLANES, moved=2 * big
    )
    arrived = across(products)
    (mine,) = call(quarter_kernel, (products[0], *arrived), (block,), moved=big)
    pieces = [mine] + [shifted(mine, "view", hop, True) for hop in range(1, PLANES)]
    (product,) = call(product_last_kernel, (*places, recv1, kept), ((GRID, PAD, NX),), moved=2 * big)
    pieces += [product] + [shifted(product, "view", hop, True) for hop in range(1, PLANES)]
    where = (plane - jnp.arange(PLANES, dtype=jnp.int32)) % PLANES
    blocks = {1: pl.BlockSpec((ROWS * NY, NX), lambda s: (s, 0))}
    for n in range(PLANES):
        blocks[2 + n] = pl.BlockSpec((*block[:2], ROWS, NX), lambda s: (0, 0, s, 0))
    (out,) = call(
        final_kernel,
        (where, est, *pieces),
        ((ZD * NY, NX),),
        ins=blocks,
        out_specs=[pl.BlockSpec((ROWS * NY, NX), lambda s: (s, 0))],
        grid=(STEPS,),
        scratch=[pltpu.VMEM((ROWS * PITCH, NX), F32)],
        moved=3 * big,
    )
    return out.reshape(estimate.shape)


def solution(mesh):
    in_specs = (
        P("slab", None, None),
        P("view", "slab", None, None),
        P("view", None, None),
        P("view", None, None),
    )
    out_specs = P("slab", None, None)

    return jax.shard_map(local, mesh=mesh, in_specs=in_specs, out_specs=out_specs, check_vma=False)
```

```python
import functools

import jax
import jax.numpy as jnp
from jax import lax
from jax.experimental import pallas as pl
from jax.experimental.pallas import tpu as pltpu
from jax.sharding import PartitionSpec as P


TAPS = 31
HALF = 15
ZD = 32
YT = 4
NX = 128
GRID = 32
NY = 128
PAD = 16
NPAD = ZD + 2 * PAD
PLANES = 4
STEPS = 4
ROWS = ZD // STEPS
PITCH = NY + 8
WORK = ZD + 8

F32 = jnp.float32
BF16 = jnp.bfloat16
VMEM = pl.BlockSpec(memory_space=pltpu.VMEM)
SMEM = pl.BlockSpec(memory_space=pltpu.SMEM)
ANY = pl.BlockSpec(memory_space=pl.ANY)


def call(kernel, operands, outs, ins=None, out_specs=None, grid=(), scratch=(), flops=0, moved=0, far=(), alias=None):
    ins = ins or {}
    in_specs = [
        ins.get(n, SMEM if jnp.issubdtype(o.dtype, jnp.integer) else VMEM) for n, o in enumerate(operands)
    ]
    return pl.pallas_call(
        kernel,
        out_shape=[(pltpu.HBM if n in far else jax.ShapeDtypeStruct)(s, F32) for n, s in enumerate(outs)],
        grid=grid,
        in_specs=in_specs,
        out_specs=out_specs or [VMEM] * len(outs),
        scratch_shapes=list(scratch),
        input_output_aliases=alias or {},
        cost_estimate=pl.CostEstimate(flops=flops, bytes_accessed=moved, transcendentals=0),
        compiler_params=pltpu.CompilerParams(vmem_limit_bytes=24 << 20),
    )(*operands)


def halves(x):
    high = x.astype(BF16)
    low = (x - high.astype(F32)).astype(BF16)
    return high, low


def dot(a, b):
    return jnp.dot(a, b, preferred_element_type=F32)


def left_dot(matrix, x):
    high, low = halves(x)
    full = dot(matrix, jnp.concatenate([high, low], axis=0))
    rows = full.shape[0] // 2
    return full[:rows] + full[rows:]


def right_dot(x, matrix):
    high, low = halves(x)
    full = dot(jnp.concatenate([high, low], axis=1), matrix)
    return full[:, :NX] + full[:, NX:]


def pack_kernel(table, last, est, send, kept0, kept1, block, turned, in_sems, out_sem, kept_sem):
    count = in_sems.shape[0]
    rows = ZD // count
    loads = []
    for n in range(count):
        part = pl.ds(n * rows * NY, rows * NY)
        loads.append(pltpu.make_async_copy(est.at[part], block.at[part], in_sems.at[n]))
        loads[-1].start()
    for n, load in enumerate(loads):
        load.wait()

        def turn(z, carry):
            at = pl.multiple_of(z * NY, NY)
            turned[pl.ds(z, NY, stride=WORK), :] = block[pl.ds(at, NY), :]
            return carry

        lax.fori_loop(n * rows, (n + 1) * rows, turn, 0, unroll=4)

    def tile(index):
        return tiles.at[pl.ds(index * YT, YT), pl.ds(0, ZD), :]

    tiles = turned.reshape(NY, WORK, NX)
    for v, kept in enumerate((kept0, kept1)):

        def step(slot, carry, v=v):
            pltpu.make_async_copy(tile(table[v, slot]), send.at[slot, v], out_sem).start()
            return carry

        lax.fori_loop(0, GRID, step, 0, unroll=4)
        pltpu.make_async_copy(tile(last[v]), kept.at[0], kept_sem.at[v]).start()
    pltpu.make_async_copy(send, send, out_sem).wait()
    for v, kept in enumerate((kept0, kept1)):
        pltpu.make_async_copy(kept, kept, kept_sem.at[v]).wait()


def unpack_kernel(v, table, recv, kept, low, high, sems):
    def put(source, c):
        at = pl.ds(pl.multiple_of(c * YT, YT), YT)
        pltpu.make_async_copy(source.at[:, pl.ds(0, PAD), :], low.at[at], sems.at[0]).start()
        pltpu.make_async_copy(source.at[:, pl.ds(PAD, PAD), :], high.at[at], sems.at[1]).start()

    def step(c, carry):
        slot = table[v, c]

        @pl.when(slot < GRID)
        def _():
            put(recv.at[slot, v], c)

        @pl.when(slot == GRID)
        def _():
            put(kept.at[0], c)

        return carry

    lax.fori_loop(0, GRID, step, 0)
    pltpu.make_async_copy(low, low, sems.at[0]).wait()
    pltpu.make_async_copy(high, high, sems.at[1]).wait()


def padded_pair(parts, *pair):
    columns = [jnp.concatenate([p[y] for p in parts], axis=0) for y in pair]
    return jnp.concatenate(columns, axis=1)


def blur_kernel(v, top, low, high, bottom, rec, zmat, xmat, ymat, ymat_t, xmat_t, out_low, out_high, work, seen_rows, sem):
    zmat, xmat, ymat, ymat_t, xmat_t = (r.at[0] for r in (zmat, xmat, ymat, ymat_t, xmat_t))
    parts = (top, low, high, bottom)
    fetch = pltpu.make_async_copy(rec.at[v], seen_rows, sem)
    fetch.start()

    def forward(group, carry):
        rows = []
        for pair in range(2):
            y = group * 4 + pair * 2
            blurred = left_dot(zmat[...], padded_pair(parts, y, y + 1))
            rows += [blurred[:, :NX], blurred[:, NX:]]
        done = right_dot(jnp.concatenate(rows, axis=0), xmat[...])
        for i in range(4):
            at = pl.multiple_of((group * 4 + i) * WORK, 8)
            work[pl.ds(at, ZD), :] = done[i * ZD : (i + 1) * ZD]
        return carry

    lax.fori_loop(0, NY // 4, forward, 0, unroll=8)
    fetch.wait()

    for base, out in ((0, out_low), (PAD, out_high)):

        def backward(step, carry, base=base, out=out):
            zz = step * 2
            z = base + zz
            x = jnp.concatenate([work[pl.ds(z + i, NY, stride=WORK), :] for i in range(2)], axis=1)
            seen = jnp.concatenate(
                [seen_rows[pl.ds(pl.multiple_of((z + i) * NY, NY), NY), :] for i in range(2)], axis=1
            )
            ratio = seen / left_dot(ymat[...], x)
            back = left_dot(ymat_t[...], ratio)
            back = right_dot(jnp.concatenate([back[:, :NX], back[:, NX:]], axis=0), xmat_t[...])
            for i in range(2):
                out[pl.ds(zz + i, NY, stride=PAD), :] = back[i * NY : (i + 1) * NY]
            return carry

        lax.fori_loop(0, PAD // 2, backward, 0, unroll=8)


def adjoint_first_kernel(v, table, top, low, high, bottom, zmat, *refs):
    parts = [p.reshape(NY // 2, PAD, NX) for p in (top, low, high, bottom)]
    send, kept = refs[-2:]
    slots = send.shape[0]
    base = pl.program_id(0) * slots

    def move(c):
        done = left_dot(zmat[v], padded_pair(parts, c * 2, c * 2 + 1))
        return done[:, :NX], done[:, NX:]

    def step(slot, carry):
        send[slot, 0, 0], send[slot, 0, 1] = move(table[v, base + slot])
        return carry

    lax.fori_loop(0, slots, step, 0, unroll=slots)

    @pl.when(pl.program_id(0) == 0)
    def _():
        kept[0], kept[1] = move(table[v, GRID])


def adjoint_last_kernel(v, table, plane, top, low, high, bottom, zmat, *refs):
    parts = [p.reshape(NY // 2, PAD, NX) for p in (top, low, high, bottom)]
    *outs, work = refs

    def step(slot, carry):
        y = table[v, slot] * 2
        done = left_dot(zmat[v], padded_pair(parts, y, y + 1))
        work[slot, pl.ds(0, ZD), :] = done[:, :NX]
        work[slot, pl.ds(ZD, ZD), :] = done[:, NX:]
        return carry

    lax.fori_loop(0, GRID + 1, step, 0, unroll=11)
    for hop, out in enumerate(outs):
        quarter = lax.rem(plane[0] + hop, PLANES)
        out[...] = work[:, pl.ds(pl.multiple_of(quarter * PAD, PAD), PAD), :]


def gather_kernel(*refs):
    *parts, send, kept, sems = refs
    copies = []
    for n, part in enumerate(parts):
        at = (n // 2, n % 2)
        copies.append(pltpu.make_async_copy(part.at[pl.ds(0, GRID)], send.at[:, at[0], at[1]], sems.at[n]))
        copies[-1].start()
    for n, part in enumerate(parts):
        kept[n // 2, n % 2] = part[GRID]
    for copy in copies:
        copy.wait()


def product_first_kernel(table, plane, recv, kept0, kept1, *outs):
    quarter = GRID // PLANES
    for hop, out in enumerate(outs):
        base = lax.rem(plane[0] + hop, PLANES) * quarter

        def step(n, carry, out=out, base=base):
            factors = []
            for v, kept in enumerate((kept0, kept1)):
                slot = table[v, base + n]
                factors.append(jnp.where(slot == GRID, kept[...], recv[jnp.minimum(slot, GRID - 1), v]))
            out[n] = factors[0] * factors[1]
            return carry

        lax.fori_loop(0, quarter, step, 0, unroll=2)


def product_last_kernel(*refs):
    *tables, recv, kept, out = refs

    def step(t, carry):
        factors = []
        for n, table in enumerate(tables):
            for v in range(2):
                slot = table[v, t]
                factors.append(jnp.where(slot == GRID, kept[n, v], recv[jnp.minimum(slot, GRID - 1), n, v]))
        while len(factors) > 1:
            factors = [a * b for a, b in zip(factors[::2], factors[1::2])]
        out[t] = factors[0]
        return carry

    lax.fori_loop(0, GRID, step, 0, unroll=4)


def quarter_kernel(first, second, third, fourth, out):
    out[...] = (first[...] * second[...]) * (third[...] * fourth[...])


def final_kernel(place, est, *refs):
    *pieces, out, turned = refs
    quarter = GRID // PLANES
    at = pl.program_id(0)
    for hop in range(PLANES):
        piece = pieces[hop]
        base = place[hop] * quarter
        for t in range(quarter):
            for j in range(2):
                turned[pl.ds((base + t) * YT + j, ROWS, stride=PITCH), :] = piece[t, j]
    for hop in range(PLANES):
        piece = pieces[PLANES + hop]
        own = place[hop]

        @pl.when(own % 2 == at // 2)
        def _(piece=piece, own=own):
            rows = pl.ds(pl.multiple_of((at % 2) * ROWS, ROWS), ROWS)
            for t in range(GRID):
                turned[pl.ds(t * YT + 2 + own // 2, ROWS, stride=PITCH), :] = piece[t, rows]

    for z in range(ROWS):
        rows = pl.ds(z * NY, NY)
        out[rows, :] = est[rows, :] * turned[pl.ds(z * PITCH, NY), :]


def stacked(matrix, axis):
    high = lax.reduce_precision(matrix, 8, 7)
    low = matrix - high
    if axis == 0:
        both = jnp.concatenate([high, low], axis=-2)
        return jnp.concatenate([both, both], axis=-1).astype(BF16)
    both = jnp.concatenate([high, low], axis=-1)
    return jnp.concatenate([both, both], axis=-2).astype(BF16)


def band(weights, positions):
    taps = jnp.arange(TAPS, dtype=jnp.int32)[None, :, None, None]
    return jnp.sum(jnp.where(positions[None, None] == taps, weights[:, :, None, None], 0.0), axis=1)


def bands(psf_taps, own):
    weights = psf_taps / jnp.sum(psf_taps, axis=-1, keepdims=True)
    i = jnp.arange(NX, dtype=jnp.int32)
    plain = band(weights[:, 1:].reshape(-1, TAPS), i[:, None] - i[None, :] + HALF)
    plain = plain / jnp.sum(plain, axis=1, keepdims=True)
    plain = plain.reshape(-1, 2, NX, NX)
    turned = plain.transpose(0, 1, 3, 2)
    ymat, xmat = turned[:, 0], plain[:, 1]
    ymat_t, xmat_t = plain[:, 0], turned[:, 1]

    wz = weights[:, 0]
    rows = own * ZD + jnp.arange(NPAD, dtype=jnp.int32) - PAD
    reach = rows[None, :] + jnp.arange(TAPS, dtype=jnp.int32)[:, None] - HALF
    inside = (reach >= 0) & (reach < GRID * ZD)
    divisor = jnp.sum(jnp.where(inside[None], wz[:, :, None], 0.0), axis=1)
    divisor = jnp.where((rows >= 0) & (rows < GRID * ZD), divisor, 1.0)
    k = jnp.arange(NPAD, dtype=jnp.int32)[None, :]
    o = jnp.arange(ZD, dtype=jnp.int32)[:, None]
    zmat = band(wz, k - o - 1) / divisor[:, PAD : PAD + ZD, None]
    zmat_t = band(wz, o - k + 2 * PAD - 1) / divisor[:, None, :]
    return (
        stacked(zmat, 0),
        stacked(xmat, 1),
        stacked(ymat, 0),
        stacked(ymat_t, 0),
        stacked(xmat_t, 1),
        stacked(zmat_t, 0),
    )


def tables(tile_map, own):
    source = tile_map // GRID
    tile = tile_map % GRID
    c = jnp.arange(GRID, dtype=jnp.int32)
    slots = jnp.arange(GRID + 1, dtype=jnp.int32)
    key = c[None, None, :] * GRID + tile
    outgoing = source == own
    pack = jnp.min(jnp.where(outgoing, key, GRID * GRID - 1), axis=2) % GRID
    inner = outgoing & (c == own)[None, :, None]
    last_key = jnp.max(jnp.where(inner, key, 0), axis=(1, 2))
    last = last_key % GRID
    own_source = lax.dynamic_index_in_dim(source, own, 1, keepdims=False)
    second = c[None, :] == (last_key // GRID)[:, None]
    place = jnp.where(second, GRID, own_source)
    chosen = jnp.sum(jnp.where(place[:, None, :] == slots[None, :, None], c[None, None, :], 0), axis=2)
    second_at = second[:, None, :] & (c == own)[None, :, None]
    value = jnp.where(second_at, GRID, c[None, :, None])
    wanted = (own * GRID + c)[None, :, None, None] == tile_map[:, None]
    arriving = jnp.sum(jnp.where(wanted, value[:, None], 0), axis=(2, 3))
    return pack, last, place, chosen, arriving


def shifted(value, axis, hop, ring):
    count = lax.axis_size(axis)
    pairs = [(i, (i + hop) % count) for i in range(count) if ring or 0 <= i + hop < count]
    return lax.ppermute(value, axis, pairs)


def exchange(value, axis):
    return lax.all_to_all(value, axis, 0, 0, tiled=True)


def after(value, *others):
    return lax.optimization_barrier((value, *others))[0]


def local(estimate, recorded, psf_taps, tile_map):
    own = lax.axis_index("slab")
    plane = lax.axis_index("view")
    pack, last, place, chosen, arriving = tables(tile_map, own)
    mats = [pltpu.with_memory_space_constraint(m, pltpu.HBM) for m in bands(psf_taps, own)]
    est = estimate.reshape(ZD * NY, NX)
    far_est = pltpu.with_memory_space_constraint(est, pltpu.HBM)
    rec = recorded.reshape(-1, ZD * NY, NX)
    strip = (NY, PAD, NX)
    big = ZD * NY * NX * 4

    def unpacked(v, recv, kept):
        return call(
            functools.partial(unpack_kernel, v),
            (place, recv, kept),
            (strip, strip),
            ins={1: ANY, 2: ANY},
            scratch=[pltpu.SemaphoreType.DMA((2,))],
            moved=2 * big,
        )

    def padded(low, high):
        return shifted(high, "slab", 1, False), low, high, shifted(low, "slab", -1, False)

    def blurred(v, parts):
        low, high = call(
            functools.partial(blur_kernel, v),
            (*parts, far_rec, *mats[:5]),
            ((NY * PAD, NX), (NY * PAD, NX)),
            ins={4: ANY}
            | {5 + n: pl.BlockSpec((1, *m.shape[1:]), lambda s: (v, 0, 0)) for n, m in enumerate(mats[:5])},
            grid=(1,),
            scratch=[
                pltpu.VMEM((NY * WORK, NX), F32),
                pltpu.VMEM((ZD * NY, NX), F32),
                pltpu.SemaphoreType.DMA,
            ],
            flops=5 << 30,
            moved=4 * big,
        )
        return low.reshape(strip), high.reshape(strip)

    far_rec = pltpu.with_memory_space_constraint(rec, pltpu.HBM)
    views = rec.shape[0]
    send, *kept = call(
        pack_kernel,
        (pack, last, far_est),
        ((GRID, views, YT, ZD, NX), (1, YT, ZD, NX), (1, YT, ZD, NX)),
        ins={2: ANY},
        out_specs=[ANY, ANY, ANY],
        scratch=[
            pltpu.VMEM((ZD * NY, NX), F32),
            pltpu.VMEM((NY * WORK, NX), F32),
            pltpu.SemaphoreType.DMA((STEPS,)),
            pltpu.SemaphoreType.DMA,
            pltpu.SemaphoreType.DMA((views,)),
        ],
        moved=2 * big,
        far=(0, 1, 2),
    )
    recv = exchange(send, "slab")
    places = [arriving] + [shifted(arriving, "view", hop, True) for hop in range(1, PLANES)]
    recv, *rest = lax.optimization_barrier((recv, *mats, *places))
    mats, places = rest[: len(mats)], rest[len(mats) :]
    parts0 = padded(*unpacked(0, recv, kept[0]))
    recv = after(recv, parts0[1])
    parts1 = padded(*unpacked(1, recv, kept[1]))
    back0 = blurred(0, parts0)
    ready0 = padded(*back0)
    parts1 = lax.optimization_barrier((*parts1, *back0))[:4]
    back1 = blurred(1, parts1)
    ready1 = padded(*back1)
    half = (GRID, views, 2, ZD, NX)

    def rows_of_tiles(at, which):
        return {at + n: pl.BlockSpec((GRID, 2, PAD, NX), lambda s: (0, which, 0, 0)) for n in range(4)}

    def adjoint_first(v, parts, buffer=None):
        operands = (chosen, *[p.reshape(GRID, YT, PAD, NX) for p in parts], mats[5])
        return call(
            functools.partial(adjoint_first_kernel, v),
            operands if buffer is None else (*operands, buffer),
            (half, (2, ZD, NX)),
            ins=rows_of_tiles(1, 0) | {6: ANY},
            out_specs=[
                pl.BlockSpec((GRID // 2, 1, 2, ZD, NX), lambda s: (s, v, 0, 0, 0)),
                pl.BlockSpec((2, ZD, NX), lambda s: (0, 0, 0)),
            ],
            grid=(2,),
            flops=1 << 30,
            moved=2 * big,
            far=(0,),
            alias={} if buffer is None else {6: 0},
        )

    def adjoint_last(v, parts):
        return call(
            functools.partial(adjoint_last_kernel, v),
            (chosen, plane.reshape(1), *[p.reshape(GRID, YT, PAD, NX) for p in parts], mats[5]),
            ((GRID + 1, PAD, NX),) * PLANES,
            ins=rows_of_tiles(2, 1),
            grid=(1,),
            scratch=[pltpu.VMEM((GRID + 1, 2 * ZD, NX), F32)],
            flops=1 << 30,
            moved=2 * big,
        )

    def across(parts):
        return [shifted(p, "view", hop, True) for hop, p in enumerate(parts) if hop]

    last0 = adjoint_last(0, ready0)
    last0 = [last0[0], *across(last0)]
    send, kept0 = adjoint_first(0, ready0)
    send, kept1 = adjoint_first(1, ready1, send)
    recv = exchange(send, "slab")
    last1 = adjoint_last(1, ready1)
    last1 = [last1[0], *across(last1)]
    send, kept = call(
        gather_kernel,
        [part for pair in zip(last0, last1) for part in pair],
        ((GRID, PLANES, views, PAD, NX), (PLANES, views, PAD, NX)),
        out_specs=[ANY, VMEM],
        scratch=[pltpu.SemaphoreType.DMA((PLANES * views,))],
        moved=2 * big,
        far=(0,),
    )
    recv1 = exchange(after(send, recv), "slab")
    block = (GRID // PLANES, 2, ZD, NX)
    products = call(
        product_first_kernel, (arriving, plane.reshape(1), recv, kept0, kept1), (block,) * PLANES, moved=2 * big
    )
    arrived = across(products)
    (mine,) = call(quarter_kernel, (products[0], *arrived), (block,), moved=big)
    pieces = [mine] + [shifted(mine, "view", hop, True) for hop in range(1, PLANES)]
    (product,) = call(product_last_kernel, (*places, recv1, kept), ((GRID, PAD, NX),), moved=2 * big)
    pieces += [product] + [shifted(product, "view", hop, True) for hop in range(1, PLANES)]
    where = (plane - jnp.arange(PLANES, dtype=jnp.int32)) % PLANES
    blocks = {1: pl.BlockSpec((ROWS * NY, NX), lambda s: (s, 0))}
    for n in range(PLANES):
        blocks[2 + n] = pl.BlockSpec((*block[:2], ROWS, NX), lambda s: (0, 0, s, 0))
    (out,) = call(
        final_kernel,
        (where, est, *pieces),
        ((ZD * NY, NX),),
        ins=blocks,
        out_specs=[pl.BlockSpec((ROWS * NY, NX), lambda s: (s, 0))],
        grid=(STEPS,),
        scratch=[pltpu.VMEM((ROWS * PITCH, NX), F32)],
        moved=3 * big,
    )
    return out.reshape(estimate.shape)


def solution(mesh):
    in_specs = (
        P("slab", None, None),
        P("view", "slab", None, None),
        P("view", None, None),
        P("view", None, None),
    )
    out_specs = P("slab", None, None)

    return jax.shard_map(local, mesh=mesh, in_specs=in_specs, out_specs=out_specs, check_vma=False)
```

```python
import functools

import jax
import jax.numpy as jnp
from jax import lax
from jax.experimental import pallas as pl
from jax.experimental.pallas import tpu as pltpu
from jax.sharding import PartitionSpec as P


TAPS = 31
HALF = 15
ZD = 32
YT = 4
NX = 128
GRID = 32
NY = 128
PAD = 16
NPAD = ZD + 2 * PAD
PLANES = 4
STEPS = 4
WIDE = 4
ROWS = ZD // STEPS
PITCH = NY + 8
WORK = ZD + 8
SLOT = PAD + 8

F32 = jnp.float32
BF16 = jnp.bfloat16
VMEM = pl.BlockSpec(memory_space=pltpu.VMEM)
SMEM = pl.BlockSpec(memory_space=pltpu.SMEM)
ANY = pl.BlockSpec(memory_space=pl.ANY)


def call(kernel, operands, outs, ins=None, out_specs=None, grid=(), scratch=(), flops=0, moved=0, far=(), alias=None):
    ins = ins or {}
    in_specs = [
        ins.get(n, SMEM if jnp.issubdtype(o.dtype, jnp.integer) else VMEM) for n, o in enumerate(operands)
    ]
    return pl.pallas_call(
        kernel,
        out_shape=[(pltpu.HBM if n in far else jax.ShapeDtypeStruct)(s, F32) for n, s in enumerate(outs)],
        grid=grid,
        in_specs=in_specs,
        out_specs=out_specs or [VMEM] * len(outs),
        scratch_shapes=list(scratch),
        input_output_aliases=alias or {},
        cost_estimate=pl.CostEstimate(flops=flops, bytes_accessed=moved, transcendentals=0),
        compiler_params=pltpu.CompilerParams(vmem_limit_bytes=24 << 20),
    )(*operands)


def halves(x):
    high = x.astype(BF16)
    low = (x - high.astype(F32)).astype(BF16)
    return high, low


def dot(a, b):
    return jnp.dot(a, b, preferred_element_type=F32)


def left_dot(matrix, x):
    high, low = halves(x)
    full = dot(matrix, jnp.concatenate([high, low], axis=0))
    rows = full.shape[0] // 2
    return full[:rows] + full[rows:]


def right_dot(x, matrix):
    high, low = halves(x)
    full = dot(jnp.concatenate([high, low], axis=1), matrix)
    return full[:, :NX] + full[:, NX:]


def pack_kernel(table, last, est, send, kept0, kept1, block, turned, in_sems, out_sem, kept_sem):
    count = in_sems.shape[0]
    rows = ZD // count
    loads = []
    for n in range(count):
        part = pl.ds(n * rows * NY, rows * NY)
        loads.append(pltpu.make_async_copy(est.at[part], block.at[part], in_sems.at[n]))
        loads[-1].start()
    for n, load in enumerate(loads):
        load.wait()

        def turn(z, carry):
            at = pl.multiple_of(z * NY, NY)
            turned[pl.ds(z, NY, stride=WORK), :] = block[pl.ds(at, NY), :]
            return carry

        lax.fori_loop(n * rows, (n + 1) * rows, turn, 0, unroll=4)

    def tile(index):
        return tiles.at[pl.ds(index * YT, YT), pl.ds(0, ZD), :]

    tiles = turned.reshape(NY, WORK, NX)
    for v, kept in enumerate((kept0, kept1)):

        def step(slot, carry, v=v):
            pltpu.make_async_copy(tile(table[v, slot]), send.at[slot, v], out_sem).start()
            return carry

        lax.fori_loop(0, GRID, step, 0, unroll=4)
        pltpu.make_async_copy(tile(last[v]), kept.at[0], kept_sem.at[v]).start()
    pltpu.make_async_copy(send, send, out_sem).wait()
    for v, kept in enumerate((kept0, kept1)):
        pltpu.make_async_copy(kept, kept, kept_sem.at[v]).wait()


def unpack_kernel(v, table, recv, kept, low, high, sems):
    def put(source, c):
        at = pl.ds(pl.multiple_of(c * YT, YT), YT)
        pltpu.make_async_copy(source.at[:, pl.ds(0, PAD), :], low.at[at], sems.at[0]).start()
        pltpu.make_async_copy(source.at[:, pl.ds(PAD, PAD), :], high.at[at], sems.at[1]).start()

    def step(c, carry):
        slot = table[v, c]

        @pl.when(slot < GRID)
        def _():
            put(recv.at[slot, v], c)

        @pl.when(slot == GRID)
        def _():
            put(kept.at[0], c)

        return carry

    lax.fori_loop(0, GRID, step, 0)
    pltpu.make_async_copy(low, low, sems.at[0]).wait()
    pltpu.make_async_copy(high, high, sems.at[1]).wait()


def padded_pair(parts, *pair):
    columns = [jnp.concatenate([p[y] for p in parts], axis=0) for y in pair]
    return jnp.concatenate(columns, axis=1)


def blur_kernel(v, top, low, high, bottom, rec, zmat, xmat, ymat, ymat_t, xmat_t, out_low, out_high, work, seen_rows, sem, done, out_sems):
    zmat, xmat, ymat, ymat_t, xmat_t = (r.at[0] for r in (zmat, xmat, ymat, ymat_t, xmat_t))
    parts = (top, low, high, bottom)
    fetch = pltpu.make_async_copy(rec.at[v], seen_rows, sem)
    fetch.start()

    def forward(group, carry):
        y = group * 4
        blurred = left_dot(zmat[...], padded_pair(parts, y, y + 1, y + 2, y + 3))
        rows = [blurred[:, i * NX : (i + 1) * NX] for i in range(4)]
        done = right_dot(jnp.concatenate(rows, axis=0), xmat[...])
        for i in range(4):
            at = pl.multiple_of((group * 4 + i) * WORK, 8)
            work[pl.ds(at, ZD), :] = done[i * ZD : (i + 1) * ZD]
        return carry

    lax.fori_loop(0, NY // 4, forward, 0, unroll=8)
    fetch.wait()

    stores = []
    for n, out in enumerate((out_low, out_high)):

        def backward(step, carry, n=n):
            zz = step * WIDE
            z = n * PAD + zz
            x = jnp.concatenate([work[pl.ds(z + i, NY, stride=WORK), :] for i in range(WIDE)], axis=1)
            seen = jnp.concatenate(
                [seen_rows[pl.ds(pl.multiple_of((z + i) * NY, NY), NY), :] for i in range(WIDE)], axis=1
            )
            ratio = seen / left_dot(ymat[...], x)
            back = left_dot(ymat_t[...], ratio)
            back = jnp.concatenate([back[:, i * NX : (i + 1) * NX] for i in range(WIDE)], axis=0)
            back = right_dot(back, xmat_t[...])
            for i in range(WIDE):
                done[n, pl.ds(zz + i, NY, stride=SLOT), :] = back[i * NY : (i + 1) * NY]
            return carry

        lax.fori_loop(0, PAD // WIDE, backward, 0, unroll=PAD // WIDE)
        rows = done.at[n].reshape(NY, SLOT, NX).at[:, pl.ds(0, PAD), :]
        stores.append(pltpu.make_async_copy(rows, out, out_sems.at[n]))
        stores[-1].start()
    for store in stores:
        store.wait()


def adjoint_first_kernel(v, table, top, low, high, bottom, zmat, *refs):
    parts = [p.reshape(NY // 2, PAD, NX) for p in (top, low, high, bottom)]
    send, kept = refs[-2:]
    slots = send.shape[0]
    base = pl.program_id(0) * slots

    def move(c):
        done = left_dot(zmat[v], padded_pair(parts, c * 2, c * 2 + 1))
        return done[:, :NX], done[:, NX:]

    def step(slot, carry):
        send[slot, 0, 0], send[slot, 0, 1] = move(table[v, base + slot])
        return carry

    lax.fori_loop(0, slots, step, 0, unroll=slots)

    @pl.when(pl.program_id(0) == 0)
    def _():
        kept[0], kept[1] = move(table[v, GRID])


def adjoint_last_kernel(v, table, plane, top, low, high, bottom, zmat, *refs):
    parts = [p.reshape(NY // 2, PAD, NX) for p in (top, low, high, bottom)]
    *outs, work = refs

    def step(slot, carry):
        y = table[v, slot] * 2
        done = left_dot(zmat[v], padded_pair(parts, y, y + 1))
        work[slot, pl.ds(0, ZD), :] = done[:, :NX]
        work[slot, pl.ds(ZD, ZD), :] = done[:, NX:]
        return carry

    lax.fori_loop(0, GRID + 1, step, 0, unroll=11)
    for hop, out in enumerate(outs):
        quarter = lax.rem(plane[0] + hop, PLANES)
        out[...] = work[:, pl.ds(pl.multiple_of(quarter * PAD, PAD), PAD), :]


def gather_kernel(*refs):
    *parts, send, kept, sems = refs
    copies = []
    for n, part in enumerate(parts):
        at = (n // 2, n % 2)
        copies.append(pltpu.make_async_copy(part.at[pl.ds(0, GRID)], send.at[:, at[0], at[1]], sems.at[n]))
        copies[-1].start()
    for n, part in enumerate(parts):
        kept[n // 2, n % 2] = part[GRID]
    for copy in copies:
        copy.wait()


def product_first_kernel(table, plane, recv, kept0, kept1, *outs):
    quarter = GRID // PLANES
    for hop, out in enumerate(outs):
        base = lax.rem(plane[0] + hop, PLANES) * quarter

        def step(n, carry, out=out, base=base):
            factors = []
            for v, kept in enumerate((kept0, kept1)):
                slot = table[v, base + n]
                factors.append(jnp.where(slot == GRID, kept[...], recv[jnp.minimum(slot, GRID - 1), v]))
            out[n] = factors[0] * factors[1]
            return carry

        lax.fori_loop(0, quarter, step, 0, unroll=2)


def product_last_kernel(*refs):
    *tables, recv, kept, out = refs

    def step(t, carry):
        factors = []
        for n, table in enumerate(tables):
            for v in range(2):
                slot = table[v, t]
                factors.append(jnp.where(slot == GRID, kept[n, v], recv[jnp.minimum(slot, GRID - 1), n, v]))
        while len(factors) > 1:
            factors = [a * b for a, b in zip(factors[::2], factors[1::2])]
        out[t] = factors[0]
        return carry

    lax.fori_loop(0, GRID, step, 0, unroll=4)


def quarter_kernel(first, second, third, fourth, out):
    out[...] = (first[...] * second[...]) * (third[...] * fourth[...])


def final_kernel(place, est, *refs):
    *pieces, out, turned = refs
    quarter = GRID // PLANES
    at = pl.program_id(0)
    for hop in range(PLANES):
        piece = pieces[hop]
        base = place[hop] * quarter
        for t in range(quarter):
            for j in range(2):
                turned[pl.ds((base + t) * YT + j, ROWS, stride=PITCH), :] = piece[t, j]
    for hop in range(PLANES):
        piece = pieces[PLANES + hop]
        own = place[hop]

        @pl.when(own % 2 == at // 2)
        def _(piece=piece, own=own):
            rows = pl.ds(pl.multiple_of((at % 2) * ROWS, ROWS), ROWS)
            for t in range(GRID):
                turned[pl.ds(t * YT + 2 + own // 2, ROWS, stride=PITCH), :] = piece[t, rows]

    for z in range(ROWS):
        rows = pl.ds(z * NY, NY)
        out[rows, :] = est[rows, :] * turned[pl.ds(z * PITCH, NY), :]


def bands_kernel(plain, xmat, ymat, ymat_t, xmat_t):
    for v in range(plain.shape[0]):
        for matrix, left, right in ((plain[v, 0], ymat_t, None), (plain[v, 1], None, xmat)):
            for _ in range(2):
                high, low = halves(matrix)
                if left is not None:
                    left[v] = jnp.concatenate([jnp.concatenate([p, p], axis=1) for p in (high, low)], axis=0)
                    left = ymat
                else:
                    right[v] = jnp.concatenate([jnp.concatenate([high, low], axis=1)] * 2, axis=0)
                    right = xmat_t
                matrix = matrix.T


def stacked(matrix):
    high = lax.reduce_precision(matrix, 8, 7)
    low = matrix - high
    both = jnp.concatenate([high, low], axis=-2)
    return jnp.concatenate([both, both], axis=-1).astype(BF16)


def band(weights, positions):
    taps = jnp.arange(TAPS, dtype=jnp.int32)[None, :, None, None]
    return jnp.sum(jnp.where(positions[None, None] == taps, weights[:, :, None, None], 0.0), axis=1)


def bands(psf_taps, own):
    weights = psf_taps / jnp.sum(psf_taps, axis=-1, keepdims=True)
    i = jnp.arange(NX, dtype=jnp.int32)
    plain = band(weights[:, 1:].reshape(-1, TAPS), i[:, None] - i[None, :] + HALF)
    plain = plain / jnp.sum(plain, axis=1, keepdims=True)
    plain = plain.reshape(-1, 2, NX, NX)
    shape = (plain.shape[0], 2 * NX, 2 * NX)
    xmat, ymat, ymat_t, xmat_t = pl.pallas_call(
        bands_kernel,
        out_shape=[jax.ShapeDtypeStruct(shape, BF16)] * 4,
        in_specs=[VMEM],
        out_specs=[VMEM] * 4,
        name="bands",
        compiler_params=pltpu.CompilerParams(vmem_limit_bytes=8 << 20),
    )(plain)

    wz = weights[:, 0]
    rows = own * ZD + jnp.arange(NPAD, dtype=jnp.int32) - PAD
    reach = rows[None, :] + jnp.arange(TAPS, dtype=jnp.int32)[:, None] - HALF
    inside = (reach >= 0) & (reach < GRID * ZD)
    divisor = jnp.sum(jnp.where(inside[None], wz[:, :, None], 0.0), axis=1)
    divisor = jnp.where((rows >= 0) & (rows < GRID * ZD), divisor, 1.0)
    k = jnp.arange(NPAD, dtype=jnp.int32)[None, :]
    o = jnp.arange(ZD, dtype=jnp.int32)[:, None]
    zmat = band(wz, k - o - 1) / divisor[:, PAD : PAD + ZD, None]
    zmat_t = band(wz, o - k + 2 * PAD - 1) / divisor[:, None, :]
    return (
        stacked(zmat),
        xmat,
        ymat,
        ymat_t,
        xmat_t,
        stacked(zmat_t),
    )


def tables(tile_map, own):
    source = tile_map // GRID
    tile = tile_map % GRID
    c = jnp.arange(GRID, dtype=jnp.int32)
    slots = jnp.arange(GRID + 1, dtype=jnp.int32)
    key = c[None, None, :] * GRID + tile
    outgoing = source == own
    pack = jnp.min(jnp.where(outgoing, key, GRID * GRID - 1), axis=2) % GRID
    inner = outgoing & (c == own)[None, :, None]
    last_key = jnp.max(jnp.where(inner, key, 0), axis=(1, 2))
    last = last_key % GRID
    own_source = lax.dynamic_index_in_dim(source, own, 1, keepdims=False)
    second = c[None, :] == (last_key // GRID)[:, None]
    place = jnp.where(second, GRID, own_source)
    chosen = jnp.sum(jnp.where(place[:, None, :] == slots[None, :, None], c[None, None, :], 0), axis=2)
    second_at = second[:, None, :] & (c == own)[None, :, None]
    value = jnp.where(second_at, GRID, c[None, :, None])
    wanted = (own * GRID + c)[None, :, None, None] == tile_map[:, None]
    arriving = jnp.sum(jnp.where(wanted, value[:, None], 0), axis=(2, 3))
    return pack, last, place, chosen, arriving


def shifted(value, axis, hop, ring):
    count = lax.axis_size(axis)
    pairs = [(i, (i + hop) % count) for i in range(count) if ring or 0 <= i + hop < count]
    return lax.ppermute(value, axis, pairs)


def exchange(value, axis):
    return lax.all_to_all(value, axis, 0, 0, tiled=True)


def after(value, *others):
    return lax.optimization_barrier((value, *others))[0]


def local(estimate, recorded, psf_taps, tile_map):
    own = lax.axis_index("slab")
    plane = lax.axis_index("view")
    pack, last, place, chosen, arriving = tables(tile_map, own)
    mats = [pltpu.with_memory_space_constraint(m, pltpu.HBM) for m in bands(psf_taps, own)]
    est = estimate.reshape(ZD * NY, NX)
    far_est = pltpu.with_memory_space_constraint(est, pltpu.HBM)
    rec = recorded.reshape(-1, ZD * NY, NX)
    strip = (NY, PAD, NX)
    big = ZD * NY * NX * 4

    def unpacked(v, recv, kept):
        return call(
            functools.partial(unpack_kernel, v),
            (place, recv, kept),
            (strip, strip),
            ins={1: ANY, 2: ANY},
            scratch=[pltpu.SemaphoreType.DMA((2,))],
            moved=2 * big,
        )

    def padded(low, high):
        return shifted(high, "slab", 1, False), low, high, shifted(low, "slab", -1, False)

    def blurred(v, parts):
        low, high = call(
            functools.partial(blur_kernel, v),
            (*parts, far_rec, *mats[:5]),
            (strip, strip),
            out_specs=[ANY, ANY],
            ins={4: ANY}
            | {5 + n: pl.BlockSpec((1, *m.shape[1:]), lambda s: (v, 0, 0)) for n, m in enumerate(mats[:5])},
            grid=(1,),
            scratch=[
                pltpu.VMEM((NY * WORK, NX), F32),
                pltpu.VMEM((ZD * NY, NX), F32),
                pltpu.SemaphoreType.DMA,
                pltpu.VMEM((2, NY * SLOT, NX), F32),
                pltpu.SemaphoreType.DMA((2,)),
            ],
            flops=5 << 30,
            moved=4 * big,
        )
        return low, high

    far_rec = pltpu.with_memory_space_constraint(rec, pltpu.HBM)
    views = rec.shape[0]
    send, *kept = call(
        pack_kernel,
        (pack, last, far_est),
        ((GRID, views, YT, ZD, NX), (1, YT, ZD, NX), (1, YT, ZD, NX)),
        ins={2: ANY},
        out_specs=[ANY, ANY, ANY],
        scratch=[
            pltpu.VMEM((ZD * NY, NX), F32),
            pltpu.VMEM((NY * WORK, NX), F32),
            pltpu.SemaphoreType.DMA((STEPS,)),
            pltpu.SemaphoreType.DMA,
            pltpu.SemaphoreType.DMA((views,)),
        ],
        moved=2 * big,
        far=(0, 1, 2),
    )
    recv = exchange(send, "slab")
    places = [arriving] + [shifted(arriving, "view", hop, True) for hop in range(1, PLANES)]
    recv, *rest = lax.optimization_barrier((recv, *mats, *places))
    mats, places = rest[: len(mats)], rest[len(mats) :]
    parts0 = padded(*unpacked(0, recv, kept[0]))
    recv = after(recv, parts0[1])
    parts1 = padded(*unpacked(1, recv, kept[1]))
    back0 = blurred(0, parts0)
    ready0 = padded(*back0)
    parts1 = lax.optimization_barrier((*parts1, *back0))[:4]
    back1 = blurred(1, parts1)
    ready1 = padded(*back1)
    half = (GRID, views, 2, ZD, NX)

    def rows_of_tiles(at, which):
        return {at + n: pl.BlockSpec((GRID, 2, PAD, NX), lambda s: (0, which, 0, 0)) for n in range(4)}

    def adjoint_first(v, parts, buffer=None):
        operands = (chosen, *[p.reshape(GRID, YT, PAD, NX) for p in parts], mats[5])
        return call(
            functools.partial(adjoint_first_kernel, v),
            operands if buffer is None else (*operands, buffer),
            (half, (2, ZD, NX)),
            ins=rows_of_tiles(1, 0) | {6: ANY},
            out_specs=[
                pl.BlockSpec((GRID // 2, 1, 2, ZD, NX), lambda s: (s, v, 0, 0, 0)),
                pl.BlockSpec((2, ZD, NX), lambda s: (0, 0, 0)),
            ],
            grid=(2,),
            flops=1 << 30,
            moved=2 * big,
            far=(0,),
            alias={} if buffer is None else {6: 0},
        )

    def adjoint_last(v, parts):
        return call(
            functools.partial(adjoint_last_kernel, v),
            (chosen, plane.reshape(1), *[p.reshape(GRID, YT, PAD, NX) for p in parts], mats[5]),
            ((GRID + 1, PAD, NX),) * PLANES,
            ins=rows_of_tiles(2, 1),
            grid=(1,),
            scratch=[pltpu.VMEM((GRID + 1, 2 * ZD, NX), F32)],
            flops=1 << 30,
            moved=2 * big,
        )

    def across(parts):
        return [shifted(p, "view", hop, True) for hop, p in enumerate(parts) if hop]

    last0 = adjoint_last(0, ready0)
    last0 = [last0[0], *across(last0)]
    send, kept0 = adjoint_first(0, ready0)
    send, kept1 = adjoint_first(1, ready1, send)
    recv = exchange(send, "slab")
    last1 = adjoint_last(1, ready1)
    last1 = [last1[0], *across(last1)]
    send, kept = call(
        gather_kernel,
        [part for pair in zip(last0, last1) for part in pair],
        ((GRID, PLANES, views, PAD, NX), (PLANES, views, PAD, NX)),
        out_specs=[ANY, VMEM],
        scratch=[pltpu.SemaphoreType.DMA((PLANES * views,))],
        moved=2 * big,
        far=(0,),
    )
    recv1 = exchange(after(send, recv), "slab")
    block = (GRID // PLANES, 2, ZD, NX)
    products = call(
        product_first_kernel, (arriving, plane.reshape(1), recv, kept0, kept1), (block,) * PLANES, moved=2 * big
    )
    arrived = across(products)
    (mine,) = call(quarter_kernel, (products[0], *arrived), (block,), moved=big)
    pieces = [mine] + [shifted(mine, "view", hop, True) for hop in range(1, PLANES)]
    (product,) = call(product_last_kernel, (*places, recv1, kept), ((GRID, PAD, NX),), moved=2 * big)
    pieces += [product] + [shifted(product, "view", hop, True) for hop in range(1, PLANES)]
    where = (plane - jnp.arange(PLANES, dtype=jnp.int32)) % PLANES
    blocks = {1: pl.BlockSpec((ROWS * NY, NX), lambda s: (s, 0))}
    for n in range(PLANES):
        blocks[2 + n] = pl.BlockSpec((*block[:2], ROWS, NX), lambda s: (0, 0, s, 0))
    (out,) = call(
        final_kernel,
        (where, est, *pieces),
        ((ZD * NY, NX),),
        ins=blocks,
        out_specs=[pl.BlockSpec((ROWS * NY, NX), lambda s: (s, 0))],
        grid=(STEPS,),
        scratch=[pltpu.VMEM((ROWS * PITCH, NX), F32)],
        moved=3 * big,
    )
    return out.reshape(estimate.shape)


def solution(mesh):
    in_specs = (
        P("slab", None, None),
        P("view", "slab", None, None),
        P("view", None, None),
        P("view", None, None),
    )
    out_specs = P("slab", None, None)

    return jax.shard_map(local, mesh=mesh, in_specs=in_specs, out_specs=out_specs, check_vma=False)
```

```python
import functools

import jax
import jax.numpy as jnp
from jax import lax
from jax.experimental import pallas as pl
from jax.experimental.pallas import tpu as pltpu
from jax.sharding import PartitionSpec as P


TAPS = 31
HALF = 15
ZD = 32
YT = 4
NX = 128
GRID = 32
NY = 128
PAD = 16
NPAD = ZD + 2 * PAD
PLANES = 4
STEPS = 4
WIDE = 8
ROWS = ZD // STEPS
PITCH = NY + 8
WORK = ZD + 8
SLOT = PAD + 8

F32 = jnp.float32
BF16 = jnp.bfloat16
VMEM = pl.BlockSpec(memory_space=pltpu.VMEM)
SMEM = pl.BlockSpec(memory_space=pltpu.SMEM)
ANY = pl.BlockSpec(memory_space=pl.ANY)


def call(kernel, operands, outs, ins=None, out_specs=None, grid=(), scratch=(), flops=0, moved=0, far=(), alias=None):
    ins = ins or {}
    in_specs = [
        ins.get(n, SMEM if jnp.issubdtype(o.dtype, jnp.integer) else VMEM) for n, o in enumerate(operands)
    ]
    return pl.pallas_call(
        kernel,
        out_shape=[(pltpu.HBM if n in far else jax.ShapeDtypeStruct)(s, F32) for n, s in enumerate(outs)],
        grid=grid,
        in_specs=in_specs,
        out_specs=out_specs or [VMEM] * len(outs),
        scratch_shapes=list(scratch),
        input_output_aliases=alias or {},
        cost_estimate=pl.CostEstimate(flops=flops, bytes_accessed=moved, transcendentals=0),
        compiler_params=pltpu.CompilerParams(vmem_limit_bytes=24 << 20),
    )(*operands)


def halves(x):
    high = x.astype(BF16)
    low = (x - high.astype(F32)).astype(BF16)
    return high, low


def dot(a, b):
    return jnp.dot(a, b, preferred_element_type=F32)


def left_dot(matrix, x):
    high, low = halves(x)
    full = dot(matrix, jnp.concatenate([high, low], axis=0))
    rows = full.shape[0] // 2
    return full[:rows] + full[rows:]


def right_dot(x, matrix):
    high, low = halves(x)
    full = dot(jnp.concatenate([high, low], axis=1), matrix)
    return full[:, :NX] + full[:, NX:]


def pack_kernel(table, last, est, send, kept0, kept1, block, turned, in_sems, out_sem, kept_sem):
    count = in_sems.shape[0]
    rows = ZD // count
    loads = []
    for n in range(count):
        part = pl.ds(n * rows * NY, rows * NY)
        loads.append(pltpu.make_async_copy(est.at[part], block.at[part], in_sems.at[n]))
        loads[-1].start()
    for n, load in enumerate(loads):
        load.wait()

        def turn(z, carry):
            at = pl.multiple_of(z * NY, NY)
            turned[pl.ds(z, NY, stride=WORK), :] = block[pl.ds(at, NY), :]
            return carry

        lax.fori_loop(n * rows, (n + 1) * rows, turn, 0, unroll=4)

    def tile(index):
        return tiles.at[pl.ds(index * YT, YT), pl.ds(0, ZD), :]

    tiles = turned.reshape(NY, WORK, NX)
    for v, kept in enumerate((kept0, kept1)):

        def step(slot, carry, v=v):
            pltpu.make_async_copy(tile(table[v, slot]), send.at[slot, v], out_sem).start()
            return carry

        lax.fori_loop(0, GRID, step, 0, unroll=4)
        pltpu.make_async_copy(tile(last[v]), kept.at[0], kept_sem.at[v]).start()
    pltpu.make_async_copy(send, send, out_sem).wait()
    for v, kept in enumerate((kept0, kept1)):
        pltpu.make_async_copy(kept, kept, kept_sem.at[v]).wait()


def unpack_kernel(v, table, recv, kept, low, high, sems):
    def put(source, c):
        at = pl.ds(pl.multiple_of(c * YT, YT), YT)
        pltpu.make_async_copy(source.at[:, pl.ds(0, PAD), :], low.at[at], sems.at[0]).start()
        pltpu.make_async_copy(source.at[:, pl.ds(PAD, PAD), :], high.at[at], sems.at[1]).start()

    def step(c, carry):
        slot = table[v, c]

        @pl.when(slot < GRID)
        def _():
            put(recv.at[slot, v], c)

        @pl.when(slot == GRID)
        def _():
            put(kept.at[0], c)

        return carry

    lax.fori_loop(0, GRID, step, 0)
    pltpu.make_async_copy(low, low, sems.at[0]).wait()
    pltpu.make_async_copy(high, high, sems.at[1]).wait()


def padded_pair(parts, *pair):
    columns = [jnp.concatenate([p[y] for p in parts], axis=0) for y in pair]
    return jnp.concatenate(columns, axis=1)


def blur_kernel(v, top, low, high, bottom, rec, zmat, xmat, ymat, ymat_t, xmat_t, out_low, out_high, work, seen_rows, sem, done, out_sems):
    zmat, xmat, ymat, ymat_t, xmat_t = (r.at[0] for r in (zmat, xmat, ymat, ymat_t, xmat_t))
    parts = (top, low, high, bottom)
    fetch = pltpu.make_async_copy(rec.at[v], seen_rows, sem)
    fetch.start()

    def forward(group, carry):
        y = group * 4
        blurred = left_dot(zmat[...], padded_pair(parts, y, y + 1, y + 2, y + 3))
        rows = [blurred[:, i * NX : (i + 1) * NX] for i in range(4)]
        done = right_dot(jnp.concatenate(rows, axis=0), xmat[...])
        for i in range(4):
            at = pl.multiple_of((group * 4 + i) * WORK, 8)
            work[pl.ds(at, ZD), :] = done[i * ZD : (i + 1) * ZD]
        return carry

    lax.fori_loop(0, NY // 4, forward, 0, unroll=8)
    fetch.wait()

    stores = []
    for n, out in enumerate((out_low, out_high)):

        def backward(step, carry, n=n):
            zz = step * WIDE
            z = n * PAD + zz
            x = jnp.concatenate([work[pl.ds(z + i, NY, stride=WORK), :] for i in range(WIDE)], axis=1)
            seen = jnp.concatenate(
                [seen_rows[pl.ds(pl.multiple_of((z + i) * NY, NY), NY), :] for i in range(WIDE)], axis=1
            )
            ratio = seen / left_dot(ymat[...], x)
            back = left_dot(ymat_t[...], ratio)
            back = jnp.concatenate([back[:, i * NX : (i + 1) * NX] for i in range(WIDE)], axis=0)
            back = right_dot(back, xmat_t[...])
            for i in range(WIDE):
                done[n, pl.ds(zz + i, NY, stride=SLOT), :] = back[i * NY : (i + 1) * NY]
            return carry

        lax.fori_loop(0, PAD // WIDE, backward, 0, unroll=PAD // WIDE)
        rows = done.at[n].reshape(NY, SLOT, NX).at[:, pl.ds(0, PAD), :]
        stores.append(pltpu.make_async_copy(rows, out, out_sems.at[n]))
        stores[-1].start()
    for store in stores:
        store.wait()


def adjoint_first_kernel(v, table, top, low, high, bottom, zmat, *refs):
    parts = [p.reshape(NY // 2, PAD, NX) for p in (top, low, high, bottom)]
    send, kept = refs[-2:]
    slots = send.shape[0]
    base = pl.program_id(0) * slots

    def move(c):
        done = left_dot(zmat[v], padded_pair(parts, c * 2, c * 2 + 1))
        return done[:, :NX], done[:, NX:]

    def step(n, carry):
        at = [table[v, base + n * 2 + i] * 2 for i in range(2)]
        done = left_dot(zmat[v], padded_pair(parts, at[0], at[0] + 1, at[1], at[1] + 1))
        for i in range(4):
            send[n * 2 + i // 2, 0, i % 2] = done[:, i * NX : (i + 1) * NX]
        return carry

    lax.fori_loop(0, slots // 2, step, 0, unroll=slots // 2)

    @pl.when(pl.program_id(0) == 0)
    def _():
        kept[0], kept[1] = move(table[v, GRID])


def adjoint_last_kernel(v, table, plane, top, low, high, bottom, zmat, *refs):
    parts = [p.reshape(NY // 2, PAD, NX) for p in (top, low, high, bottom)]
    *outs, work = refs

    def put(*slots):
        at = [table[v, slot] * 2 for slot in slots]
        done = left_dot(zmat[v], padded_pair(parts, *[y + i for y in at for i in range(2)]))
        for n, slot in enumerate(slots):
            for i in range(2):
                first = (2 * n + i) * NX
                work[slot, pl.ds(i * ZD, ZD), :] = done[:, first : first + NX]

    def step(n, carry):
        put(n * 2, n * 2 + 1)
        return carry

    lax.fori_loop(0, GRID // 2, step, 0, unroll=8)
    put(GRID)
    for hop, out in enumerate(outs):
        quarter = lax.rem(plane[0] + hop, PLANES)
        out[...] = work[:, pl.ds(pl.multiple_of(quarter * PAD, PAD), PAD), :]


def gather_kernel(*refs):
    *parts, send, kept, sems = refs
    copies = []
    for n, part in enumerate(parts):
        at = (n // 2, n % 2)
        copies.append(pltpu.make_async_copy(part.at[pl.ds(0, GRID)], send.at[:, at[0], at[1]], sems.at[n]))
        copies[-1].start()
    for n, part in enumerate(parts):
        kept[n // 2, n % 2] = part[GRID]
    for copy in copies:
        copy.wait()


def product_first_kernel(table, plane, recv, kept0, kept1, *outs):
    quarter = GRID // PLANES
    for hop, out in enumerate(outs):
        base = lax.rem(plane[0] + hop, PLANES) * quarter

        def step(n, carry, out=out, base=base):
            factors = []
            for v, kept in enumerate((kept0, kept1)):
                slot = table[v, base + n]
                factors.append(jnp.where(slot == GRID, kept[...], recv[jnp.minimum(slot, GRID - 1), v]))
            out[n] = factors[0] * factors[1]
            return carry

        lax.fori_loop(0, quarter, step, 0, unroll=2)


def product_last_kernel(*refs):
    *tables, recv, kept, out = refs

    def step(t, carry):
        factors = []
        for n, table in enumerate(tables):
            for v in range(2):
                slot = table[v, t]
                factors.append(jnp.where(slot == GRID, kept[n, v], recv[jnp.minimum(slot, GRID - 1), n, v]))
        while len(factors) > 1:
            factors = [a * b for a, b in zip(factors[::2], factors[1::2])]
        out[t] = factors[0]
        return carry

    lax.fori_loop(0, GRID, step, 0, unroll=4)


def quarter_kernel(first, second, third, fourth, out):
    out[...] = (first[...] * second[...]) * (third[...] * fourth[...])


def final_kernel(place, est, *refs):
    *pieces, out, turned = refs
    quarter = GRID // PLANES
    at = pl.program_id(0)
    for hop in range(PLANES):
        piece = pieces[hop]
        base = place[hop] * quarter
        for t in range(quarter):
            for j in range(2):
                turned[pl.ds((base + t) * YT + j, ROWS, stride=PITCH), :] = piece[t, j]
    for hop in range(PLANES):
        piece = pieces[PLANES + hop]
        own = place[hop]

        @pl.when(own % 2 == at // 2)
        def _(piece=piece, own=own):
            rows = pl.ds(pl.multiple_of((at % 2) * ROWS, ROWS), ROWS)
            for t in range(GRID):
                turned[pl.ds(t * YT + 2 + own // 2, ROWS, stride=PITCH), :] = piece[t, rows]

    for z in range(ROWS):
        rows = pl.ds(z * NY, NY)
        out[rows, :] = est[rows, :] * turned[pl.ds(z * PITCH, NY), :]


def bands_kernel(plain, xmat, ymat, ymat_t, xmat_t):
    for v in range(plain.shape[0]):
        for matrix, left, right in ((plain[v, 0], ymat_t, None), (plain[v, 1], None, xmat)):
            for _ in range(2):
                high, low = halves(matrix)
                if left is not None:
                    left[v] = jnp.concatenate([jnp.concatenate([p, p], axis=1) for p in (high, low)], axis=0)
                    left = ymat
                else:
                    right[v] = jnp.concatenate([jnp.concatenate([high, low], axis=1)] * 2, axis=0)
                    right = xmat_t
                matrix = matrix.T


def stacked(matrix):
    high = lax.reduce_precision(matrix, 8, 7)
    low = matrix - high
    both = jnp.concatenate([high, low], axis=-2)
    return jnp.concatenate([both, both], axis=-1).astype(BF16)


def band(weights, positions):
    taps = jnp.arange(TAPS, dtype=jnp.int32)[None, :, None, None]
    return jnp.sum(jnp.where(positions[None, None] == taps, weights[:, :, None, None], 0.0), axis=1)


def bands(psf_taps, own):
    weights = psf_taps / jnp.sum(psf_taps, axis=-1, keepdims=True)
    i = jnp.arange(NX, dtype=jnp.int32)
    plain = band(weights[:, 1:].reshape(-1, TAPS), i[:, None] - i[None, :] + HALF)
    plain = plain / jnp.sum(plain, axis=1, keepdims=True)
    plain = plain.reshape(-1, 2, NX, NX)
    shape = (plain.shape[0], 2 * NX, 2 * NX)
    xmat, ymat, ymat_t, xmat_t = pl.pallas_call(
        bands_kernel,
        out_shape=[jax.ShapeDtypeStruct(shape, BF16)] * 4,
        in_specs=[VMEM],
        out_specs=[VMEM] * 4,
        name="bands",
        compiler_params=pltpu.CompilerParams(vmem_limit_bytes=8 << 20),
    )(plain)

    wz = weights[:, 0]
    rows = own * ZD + jnp.arange(NPAD, dtype=jnp.int32) - PAD
    reach = rows[None, :] + jnp.arange(TAPS, dtype=jnp.int32)[:, None] - HALF
    inside = (reach >= 0) & (reach < GRID * ZD)
    divisor = jnp.sum(jnp.where(inside[None], wz[:, :, None], 0.0), axis=1)
    divisor = jnp.where((rows >= 0) & (rows < GRID * ZD), divisor, 1.0)
    k = jnp.arange(NPAD, dtype=jnp.int32)[None, :]
    o = jnp.arange(ZD, dtype=jnp.int32)[:, None]
    zmat = band(wz, k - o - 1) / divisor[:, PAD : PAD + ZD, None]
    zmat_t = band(wz, o - k + 2 * PAD - 1) / divisor[:, None, :]
    return (
        stacked(zmat),
        xmat,
        ymat,
        ymat_t,
        xmat_t,
        stacked(zmat_t),
    )


def tables(tile_map, own):
    source = tile_map // GRID
    tile = tile_map % GRID
    c = jnp.arange(GRID, dtype=jnp.int32)
    slots = jnp.arange(GRID + 1, dtype=jnp.int32)
    key = c[None, None, :] * GRID + tile
    outgoing = source == own
    pack = jnp.min(jnp.where(outgoing, key, GRID * GRID - 1), axis=2) % GRID
    inner = outgoing & (c == own)[None, :, None]
    last_key = jnp.max(jnp.where(inner, key, 0), axis=(1, 2))
    last = last_key % GRID
    own_source = lax.dynamic_index_in_dim(source, own, 1, keepdims=False)
    second = c[None, :] == (last_key // GRID)[:, None]
    place = jnp.where(second, GRID, own_source)
    chosen = jnp.sum(jnp.where(place[:, None, :] == slots[None, :, None], c[None, None, :], 0), axis=2)
    second_at = second[:, None, :] & (c == own)[None, :, None]
    value = jnp.where(second_at, GRID, c[None, :, None])
    wanted = (own * GRID + c)[None, :, None, None] == tile_map[:, None]
    arriving = jnp.sum(jnp.where(wanted, value[:, None], 0), axis=(2, 3))
    return pack, last, place, chosen, arriving


def shifted(value, axis, hop, ring):
    count = lax.axis_size(axis)
    pairs = [(i, (i + hop) % count) for i in range(count) if ring or 0 <= i + hop < count]
    return lax.ppermute(value, axis, pairs)


def exchange(value, axis):
    return lax.all_to_all(value, axis, 0, 0, tiled=True)


def after(value, *others):
    return lax.optimization_barrier((value, *others))[0]


def local(estimate, recorded, psf_taps, tile_map):
    own = lax.axis_index("slab")
    plane = lax.axis_index("view")
    pack, last, place, chosen, arriving = tables(tile_map, own)
    mats = [pltpu.with_memory_space_constraint(m, pltpu.HBM) for m in bands(psf_taps, own)]
    est = estimate.reshape(ZD * NY, NX)
    far_est = pltpu.with_memory_space_constraint(est, pltpu.HBM)
    rec = recorded.reshape(-1, ZD * NY, NX)
    strip = (NY, PAD, NX)
    big = ZD * NY * NX * 4

    def unpacked(v, recv, kept):
        return call(
            functools.partial(unpack_kernel, v),
            (place, recv, kept),
            (strip, strip),
            ins={1: ANY, 2: ANY},
            scratch=[pltpu.SemaphoreType.DMA((2,))],
            moved=2 * big,
        )

    def padded(low, high):
        return shifted(high, "slab", 1, False), low, high, shifted(low, "slab", -1, False)

    def blurred(v, parts):
        low, high = call(
            functools.partial(blur_kernel, v),
            (*parts, far_rec, *mats[:5]),
            (strip, strip),
            out_specs=[ANY, ANY],
            ins={4: ANY}
            | {5 + n: pl.BlockSpec((1, *m.shape[1:]), lambda s: (v, 0, 0)) for n, m in enumerate(mats[:5])},
            grid=(1,),
            scratch=[
                pltpu.VMEM((NY * WORK, NX), F32),
                pltpu.VMEM((ZD * NY, NX), F32),
                pltpu.SemaphoreType.DMA,
                pltpu.VMEM((2, NY * SLOT, NX), F32),
                pltpu.SemaphoreType.DMA((2,)),
            ],
            flops=5 << 30,
            moved=4 * big,
        )
        return low, high

    far_rec = pltpu.with_memory_space_constraint(rec, pltpu.HBM)
    views = rec.shape[0]
    send, *kept = call(
        pack_kernel,
        (pack, last, far_est),
        ((GRID, views, YT, ZD, NX), (1, YT, ZD, NX), (1, YT, ZD, NX)),
        ins={2: ANY},
        out_specs=[ANY, ANY, ANY],
        scratch=[
            pltpu.VMEM((ZD * NY, NX), F32),
            pltpu.VMEM((NY * WORK, NX), F32),
            pltpu.SemaphoreType.DMA((STEPS,)),
            pltpu.SemaphoreType.DMA,
            pltpu.SemaphoreType.DMA((views,)),
        ],
        moved=2 * big,
        far=(0, 1, 2),
    )
    recv = exchange(send, "slab")
    places = [arriving] + [shifted(arriving, "view", hop, True) for hop in range(1, PLANES)]
    recv, *rest = lax.optimization_barrier((recv, *mats, *places))
    mats, places = rest[: len(mats)], rest[len(mats) :]
    parts0 = padded(*unpacked(0, recv, kept[0]))
    recv = after(recv, parts0[1])
    parts1 = padded(*unpacked(1, recv, kept[1]))
    back0 = blurred(0, parts0)
    ready0 = padded(*back0)
    parts1 = lax.optimization_barrier((*parts1, *back0))[:4]
    back1 = blurred(1, parts1)
    ready1 = padded(*back1)
    half = (GRID, views, 2, ZD, NX)

    def rows_of_tiles(at, which):
        return {at + n: pl.BlockSpec((GRID, 2, PAD, NX), lambda s: (0, which, 0, 0)) for n in range(4)}

    def adjoint_first(v, parts, buffer=None):
        operands = (chosen, *[p.reshape(GRID, YT, PAD, NX) for p in parts], mats[5])
        return call(
            functools.partial(adjoint_first_kernel, v),
            operands if buffer is None else (*operands, buffer),
            (half, (2, ZD, NX)),
            ins=rows_of_tiles(1, 0) | {6: ANY},
            out_specs=[
                pl.BlockSpec((GRID // 2, 1, 2, ZD, NX), lambda s: (s, v, 0, 0, 0)),
                pl.BlockSpec((2, ZD, NX), lambda s: (0, 0, 0)),
            ],
            grid=(2,),
            flops=1 << 30,
            moved=2 * big,
            far=(0,),
            alias={} if buffer is None else {6: 0},
        )

    def adjoint_last(v, parts):
        return call(
            functools.partial(adjoint_last_kernel, v),
            (chosen, plane.reshape(1), *[p.reshape(GRID, YT, PAD, NX) for p in parts], mats[5]),
            ((GRID + 1, PAD, NX),) * PLANES,
            ins=rows_of_tiles(2, 1),
            grid=(1,),
            scratch=[pltpu.VMEM((GRID + 1, 2 * ZD, NX), F32)],
            flops=1 << 30,
            moved=2 * big,
        )

    def across(parts):
        return [shifted(p, "view", hop, True) for hop, p in enumerate(parts) if hop]

    last0 = adjoint_last(0, ready0)
    last0 = [last0[0], *across(last0)]
    send, kept0 = adjoint_first(0, ready0)
    send, kept1 = adjoint_first(1, ready1, send)
    recv = exchange(send, "slab")
    last1 = adjoint_last(1, ready1)
    last1 = [last1[0], *across(last1)]
    send, kept = call(
        gather_kernel,
        [part for pair in zip(last0, last1) for part in pair],
        ((GRID, PLANES, views, PAD, NX), (PLANES, views, PAD, NX)),
        out_specs=[ANY, VMEM],
        scratch=[pltpu.SemaphoreType.DMA((PLANES * views,))],
        moved=2 * big,
        far=(0,),
    )
    recv1 = exchange(after(send, recv), "slab")
    block = (GRID // PLANES, 2, ZD, NX)
    products = call(
        product_first_kernel, (arriving, plane.reshape(1), recv, kept0, kept1), (block,) * PLANES, moved=2 * big
    )
    arrived = across(products)
    (mine,) = call(quarter_kernel, (products[0], *arrived), (block,), moved=big)
    pieces = [mine] + [shifted(mine, "view", hop, True) for hop in range(1, PLANES)]
    (product,) = call(product_last_kernel, (*places, recv1, kept), ((GRID, PAD, NX),), moved=2 * big)
    pieces += [product] + [shifted(product, "view", hop, True) for hop in range(1, PLANES)]
    where = (plane - jnp.arange(PLANES, dtype=jnp.int32)) % PLANES
    blocks = {1: pl.BlockSpec((ROWS * NY, NX), lambda s: (s, 0))}
    for n in range(PLANES):
        blocks[2 + n] = pl.BlockSpec((*block[:2], ROWS, NX), lambda s: (0, 0, s, 0))
    (out,) = call(
        final_kernel,
        (where, est, *pieces),
        ((ZD * NY, NX),),
        ins=blocks,
        out_specs=[pl.BlockSpec((ROWS * NY, NX), lambda s: (s, 0))],
        grid=(STEPS,),
        scratch=[pltpu.VMEM((ROWS * PITCH, NX), F32)],
        moved=3 * big,
    )
    return out.reshape(estimate.shape)


def solution(mesh):
    in_specs = (
        P("slab", None, None),
        P("view", "slab", None, None),
        P("view", None, None),
        P("view", None, None),
    )
    out_specs = P("slab", None, None)

    return jax.shard_map(local, mesh=mesh, in_specs=in_specs, out_specs=out_specs, check_vma=False)
```

```python
import functools

import jax
import jax.numpy as jnp
from jax import lax
from jax.experimental import pallas as pl
from jax.experimental.pallas import tpu as pltpu
from jax.sharding import PartitionSpec as P


TAPS = 31
HALF = 15
ZD = 32
YT = 4
NX = 128
GRID = 32
NY = 128
PAD = 16
NPAD = ZD + 2 * PAD
PLANES = 4
STEPS = 4
WIDE = 8
ROWS = ZD // STEPS
PITCH = NY + 8
WORK = ZD + 8
SLOT = PAD + 8

F32 = jnp.float32
BF16 = jnp.bfloat16
VMEM = pl.BlockSpec(memory_space=pltpu.VMEM)
SMEM = pl.BlockSpec(memory_space=pltpu.SMEM)
ANY = pl.BlockSpec(memory_space=pl.ANY)


def call(kernel, operands, outs, ins=None, out_specs=None, grid=(), scratch=(), flops=0, moved=0, far=(), alias=None):
    ins = ins or {}
    in_specs = [
        ins.get(n, SMEM if jnp.issubdtype(o.dtype, jnp.integer) else VMEM) for n, o in enumerate(operands)
    ]
    return pl.pallas_call(
        kernel,
        out_shape=[(pltpu.HBM if n in far else jax.ShapeDtypeStruct)(s, F32) for n, s in enumerate(outs)],
        grid=grid,
        in_specs=in_specs,
        out_specs=out_specs or [VMEM] * len(outs),
        scratch_shapes=list(scratch),
        input_output_aliases=alias or {},
        cost_estimate=pl.CostEstimate(flops=flops, bytes_accessed=moved, transcendentals=0),
        compiler_params=pltpu.CompilerParams(vmem_limit_bytes=24 << 20),
    )(*operands)


def halves(x):
    high = x.astype(BF16)
    low = (x - high.astype(F32)).astype(BF16)
    return high, low


def dot(a, b):
    return jnp.dot(a, b, preferred_element_type=F32)


def left_dot(matrix, x):
    high, low = halves(x)
    full = dot(matrix, jnp.concatenate([high, low], axis=0))
    rows = full.shape[0] // 2
    return full[:rows] + full[rows:]


def right_dot(x, matrix):
    high, low = halves(x)
    full = dot(jnp.concatenate([high, low], axis=1), matrix)
    return full[:, :NX] + full[:, NX:]


def pack_kernel(table, last, est, send, kept0, kept1, block, turned, in_sems, out_sem, kept_sem):
    count = in_sems.shape[0]
    rows = ZD // count
    loads = []
    for n in range(count):
        part = pl.ds(n * rows * NY, rows * NY)
        loads.append(pltpu.make_async_copy(est.at[part], block.at[part], in_sems.at[n]))
        loads[-1].start()
    for n, load in enumerate(loads):
        load.wait()

        def turn(z, carry):
            at = pl.multiple_of(z * NY, NY)
            turned[pl.ds(z, NY, stride=WORK), :] = block[pl.ds(at, NY), :]
            return carry

        lax.fori_loop(n * rows, (n + 1) * rows, turn, 0, unroll=4)

    def tile(index):
        return tiles.at[pl.ds(index * YT, YT), pl.ds(0, ZD), :]

    tiles = turned.reshape(NY, WORK, NX)
    for v, kept in enumerate((kept0, kept1)):

        def step(slot, carry, v=v):
            pltpu.make_async_copy(tile(table[v, slot]), send.at[slot, v], out_sem).start()
            return carry

        lax.fori_loop(0, GRID, step, 0, unroll=4)
        pltpu.make_async_copy(tile(last[v]), kept.at[0], kept_sem.at[v]).start()
    pltpu.make_async_copy(send, send, out_sem).wait()
    for v, kept in enumerate((kept0, kept1)):
        pltpu.make_async_copy(kept, kept, kept_sem.at[v]).wait()


def unpack_kernel(v, table, recv, kept, low, high, sems):
    def put(source, c):
        at = pl.ds(pl.multiple_of(c * YT, YT), YT)
        pltpu.make_async_copy(source.at[:, pl.ds(0, PAD), :], low.at[at], sems.at[0]).start()
        pltpu.make_async_copy(source.at[:, pl.ds(PAD, PAD), :], high.at[at], sems.at[1]).start()

    def step(c, carry):
        slot = table[v, c]

        @pl.when(slot < GRID)
        def _():
            put(recv.at[slot, v], c)

        @pl.when(slot == GRID)
        def _():
            put(kept.at[0], c)

        return carry

    lax.fori_loop(0, GRID, step, 0)
    pltpu.make_async_copy(low, low, sems.at[0]).wait()
    pltpu.make_async_copy(high, high, sems.at[1]).wait()


def padded_pair(parts, *pair):
    columns = [jnp.concatenate([p[y] for p in parts], axis=0) for y in pair]
    return jnp.concatenate(columns, axis=1)


def blur_kernel(v, top, low, high, bottom, rec, zmat, xmat, ymat, ymat_t, xmat_t, out_low, out_high, work, seen_rows, sem, done, out_sems):
    zmat, xmat, ymat, ymat_t, xmat_t = (r.at[0] for r in (zmat, xmat, ymat, ymat_t, xmat_t))
    parts = (top, low, high, bottom)
    fetch = pltpu.make_async_copy(rec.at[v], seen_rows, sem)
    fetch.start()

    def forward(group, carry):
        y = group * 4
        blurred = left_dot(zmat[...], padded_pair(parts, y, y + 1, y + 2, y + 3))
        rows = [blurred[:, i * NX : (i + 1) * NX] for i in range(4)]
        done = right_dot(jnp.concatenate(rows, axis=0), xmat[...])
        for i in range(4):
            at = pl.multiple_of((group * 4 + i) * WORK, 8)
            work[pl.ds(at, ZD), :] = done[i * ZD : (i + 1) * ZD]
        return carry

    lax.fori_loop(0, NY // 4, forward, 0, unroll=16)
    fetch.wait()

    stores = []
    for n, out in enumerate((out_low, out_high)):

        def backward(step, carry, n=n):
            zz = step * WIDE
            z = n * PAD + zz
            x = jnp.concatenate([work[pl.ds(z + i, NY, stride=WORK), :] for i in range(WIDE)], axis=1)
            seen = jnp.concatenate(
                [seen_rows[pl.ds(pl.multiple_of((z + i) * NY, NY), NY), :] for i in range(WIDE)], axis=1
            )
            ratio = seen / left_dot(ymat[...], x)
            back = left_dot(ymat_t[...], ratio)
            back = jnp.concatenate([back[:, i * NX : (i + 1) * NX] for i in range(WIDE)], axis=0)
            back = right_dot(back, xmat_t[...])
            for i in range(WIDE):
                done[n, pl.ds(zz + i, NY, stride=SLOT), :] = back[i * NY : (i + 1) * NY]
            return carry

        lax.fori_loop(0, PAD // WIDE, backward, 0, unroll=PAD // WIDE)
        rows = done.at[n].reshape(NY, SLOT, NX).at[:, pl.ds(0, PAD), :]
        stores.append(pltpu.make_async_copy(rows, out, out_sems.at[n]))
        stores[-1].start()
    for store in stores:
        store.wait()


def adjoint_first_kernel(v, table, top, low, high, bottom, zmat, *refs):
    parts = [p.reshape(NY // 2, PAD, NX) for p in (top, low, high, bottom)]
    send, kept = refs[-2:]
    slots = send.shape[0]
    base = pl.program_id(0) * slots

    def move(c):
        done = left_dot(zmat[v], padded_pair(parts, c * 2, c * 2 + 1))
        return done[:, :NX], done[:, NX:]

    def step(n, carry):
        at = [table[v, base + n * 2 + i] * 2 for i in range(2)]
        done = left_dot(zmat[v], padded_pair(parts, at[0], at[0] + 1, at[1], at[1] + 1))
        for i in range(4):
            send[n * 2 + i // 2, 0, i % 2] = done[:, i * NX : (i + 1) * NX]
        return carry

    lax.fori_loop(0, slots // 2, step, 0, unroll=slots // 2)

    @pl.when(pl.program_id(0) == 0)
    def _():
        kept[0], kept[1] = move(table[v, GRID])


def adjoint_last_kernel(v, table, plane, top, low, high, bottom, zmat, *refs):
    parts = [p.reshape(NY // 2, PAD, NX) for p in (top, low, high, bottom)]
    *outs, work = refs

    def put(*slots):
        at = [table[v, slot] * 2 for slot in slots]
        done = left_dot(zmat[v], padded_pair(parts, *[y + i for y in at for i in range(2)]))
        for n, slot in enumerate(slots):
            for i in range(2):
                first = (2 * n + i) * NX
                work[slot, pl.ds(i * ZD, ZD), :] = done[:, first : first + NX]

    def step(n, carry):
        put(n * 2, n * 2 + 1)
        return carry

    lax.fori_loop(0, GRID // 2, step, 0, unroll=8)
    put(GRID)
    for hop, out in enumerate(outs):
        quarter = lax.rem(plane[0] + hop, PLANES)
        out[...] = work[:, pl.ds(pl.multiple_of(quarter * PAD, PAD), PAD), :]


def gather_kernel(*refs):
    *parts, send, kept, sems = refs
    copies = []
    for n, part in enumerate(parts):
        at = (n // 2, n % 2)
        copies.append(pltpu.make_async_copy(part.at[pl.ds(0, GRID)], send.at[:, at[0], at[1]], sems.at[n]))
        copies[-1].start()
    for n, part in enumerate(parts):
        kept[n // 2, n % 2] = part[GRID]
    for copy in copies:
        copy.wait()


def product_first_kernel(table, plane, recv, kept0, kept1, *outs):
    quarter = GRID // PLANES
    for hop, out in enumerate(outs):
        base = lax.rem(plane[0] + hop, PLANES) * quarter

        def step(n, carry, out=out, base=base):
            factors = []
            for v, kept in enumerate((kept0, kept1)):
                slot = table[v, base + n]
                factors.append(jnp.where(slot == GRID, kept[...], recv[jnp.minimum(slot, GRID - 1), v]))
            out[n] = factors[0] * factors[1]
            return carry

        lax.fori_loop(0, quarter, step, 0, unroll=8)


def product_last_kernel(*refs):
    *tables, recv, kept, out = refs

    def step(t, carry):
        factors = []
        for n, table in enumerate(tables):
            for v in range(2):
                slot = table[v, t]
                factors.append(jnp.where(slot == GRID, kept[n, v], recv[jnp.minimum(slot, GRID - 1), n, v]))
        while len(factors) > 1:
            factors = [a * b for a, b in zip(factors[::2], factors[1::2])]
        out[t] = factors[0]
        return carry

    lax.fori_loop(0, GRID, step, 0, unroll=8)


def quarter_kernel(first, second, third, fourth, out):
    out[...] = (first[...] * second[...]) * (third[...] * fourth[...])


def final_kernel(place, est, *refs):
    *pieces, out, turned = refs
    quarter = GRID // PLANES
    at = pl.program_id(0)
    for hop in range(PLANES):
        piece = pieces[hop]
        base = place[hop] * quarter
        for t in range(quarter):
            for j in range(2):
                turned[pl.ds((base + t) * YT + j, ROWS, stride=PITCH), :] = piece[t, j]
    for hop in range(PLANES):
        piece = pieces[PLANES + hop]
        own = place[hop]

        @pl.when(own % 2 == at // 2)
        def _(piece=piece, own=own):
            rows = pl.ds(pl.multiple_of((at % 2) * ROWS, ROWS), ROWS)
            for t in range(GRID):
                turned[pl.ds(t * YT + 2 + own // 2, ROWS, stride=PITCH), :] = piece[t, rows]

    for z in range(ROWS):
        rows = pl.ds(z * NY, NY)
        out[rows, :] = est[rows, :] * turned[pl.ds(z * PITCH, NY), :]


def bands_kernel(plain, xmat, ymat, ymat_t, xmat_t):
    for v in range(plain.shape[0]):
        for matrix, left, right in ((plain[v, 0], ymat_t, None), (plain[v, 1], None, xmat)):
            for _ in range(2):
                high, low = halves(matrix)
                if left is not None:
                    left[v] = jnp.concatenate([jnp.concatenate([p, p], axis=1) for p in (high, low)], axis=0)
                    left = ymat
                else:
                    right[v] = jnp.concatenate([jnp.concatenate([high, low], axis=1)] * 2, axis=0)
                    right = xmat_t
                matrix = matrix.T


def stacked(matrix):
    high = lax.reduce_precision(matrix, 8, 7)
    low = matrix - high
    both = jnp.concatenate([high, low], axis=-2)
    return jnp.concatenate([both, both], axis=-1).astype(BF16)


def band(weights, positions):
    taps = jnp.arange(TAPS, dtype=jnp.int32)[None, :, None, None]
    return jnp.sum(jnp.where(positions[None, None] == taps, weights[:, :, None, None], 0.0), axis=1)


def bands(psf_taps, own):
    weights = psf_taps / jnp.sum(psf_taps, axis=-1, keepdims=True)
    i = jnp.arange(NX, dtype=jnp.int32)
    plain = band(weights[:, 1:].reshape(-1, TAPS), i[:, None] - i[None, :] + HALF)
    plain = plain / jnp.sum(plain, axis=1, keepdims=True)
    plain = plain.reshape(-1, 2, NX, NX)
    shape = (plain.shape[0], 2 * NX, 2 * NX)
    xmat, ymat, ymat_t, xmat_t = pl.pallas_call(
        bands_kernel,
        out_shape=[jax.ShapeDtypeStruct(shape, BF16)] * 4,
        in_specs=[VMEM],
        out_specs=[VMEM] * 4,
        name="bands",
        compiler_params=pltpu.CompilerParams(vmem_limit_bytes=8 << 20),
    )(plain)

    wz = weights[:, 0]
    rows = own * ZD + jnp.arange(NPAD, dtype=jnp.int32) - PAD
    reach = rows[None, :] + jnp.arange(TAPS, dtype=jnp.int32)[:, None] - HALF
    inside = (reach >= 0) & (reach < GRID * ZD)
    divisor = jnp.sum(jnp.where(inside[None], wz[:, :, None], 0.0), axis=1)
    divisor = jnp.where((rows >= 0) & (rows < GRID * ZD), divisor, 1.0)
    k = jnp.arange(NPAD, dtype=jnp.int32)[None, :]
    o = jnp.arange(ZD, dtype=jnp.int32)[:, None]
    zmat = band(wz, k - o - 1) / divisor[:, PAD : PAD + ZD, None]
    zmat_t = band(wz, o - k + 2 * PAD - 1) / divisor[:, None, :]
    return (
        stacked(zmat),
        xmat,
        ymat,
        ymat_t,
        xmat_t,
        stacked(zmat_t),
    )


def tables(tile_map, own):
    source = tile_map // GRID
    tile = tile_map % GRID
    c = jnp.arange(GRID, dtype=jnp.int32)
    slots = jnp.arange(GRID + 1, dtype=jnp.int32)
    key = c[None, None, :] * GRID + tile
    outgoing = source == own
    pack = jnp.min(jnp.where(outgoing, key, GRID * GRID - 1), axis=2) % GRID
    inner = outgoing & (c == own)[None, :, None]
    last_key = jnp.max(jnp.where(inner, key, 0), axis=(1, 2))
    last = last_key % GRID
    own_source = lax.dynamic_index_in_dim(source, own, 1, keepdims=False)
    second = c[None, :] == (last_key // GRID)[:, None]
    place = jnp.where(second, GRID, own_source)
    chosen = jnp.sum(jnp.where(place[:, None, :] == slots[None, :, None], c[None, None, :], 0), axis=2)
    second_at = second[:, None, :] & (c == own)[None, :, None]
    value = jnp.where(second_at, GRID, c[None, :, None])
    wanted = (own * GRID + c)[None, :, None, None] == tile_map[:, None]
    arriving = jnp.sum(jnp.where(wanted, value[:, None], 0), axis=(2, 3))
    return pack, last, place, chosen, arriving


def shifted(value, axis, hop, ring):
    count = lax.axis_size(axis)
    pairs = [(i, (i + hop) % count) for i in range(count) if ring or 0 <= i + hop < count]
    return lax.ppermute(value, axis, pairs)


def exchange(value, axis):
    return lax.all_to_all(value, axis, 0, 0, tiled=True)


def after(value, *others):
    return lax.optimization_barrier((value, *others))[0]


def local(estimate, recorded, psf_taps, tile_map):
    own = lax.axis_index("slab")
    plane = lax.axis_index("view")
    pack, last, place, chosen, arriving = tables(tile_map, own)
    mats = [pltpu.with_memory_space_constraint(m, pltpu.HBM) for m in bands(psf_taps, own)]
    est = estimate.reshape(ZD * NY, NX)
    far_est = pltpu.with_memory_space_constraint(est, pltpu.HBM)
    rec = recorded.reshape(-1, ZD * NY, NX)
    strip = (NY, PAD, NX)
    big = ZD * NY * NX * 4

    def unpacked(v, recv, kept):
        return call(
            functools.partial(unpack_kernel, v),
            (place, recv, kept),
            (strip, strip),
            ins={1: ANY, 2: ANY},
            scratch=[pltpu.SemaphoreType.DMA((2,))],
            moved=2 * big,
        )

    def padded(low, high):
        return shifted(high, "slab", 1, False), low, high, shifted(low, "slab", -1, False)

    def blurred(v, parts):
        low, high = call(
            functools.partial(blur_kernel, v),
            (*parts, far_rec, *mats[:5]),
            (strip, strip),
            out_specs=[ANY, ANY],
            ins={4: ANY}
            | {5 + n: pl.BlockSpec((1, *m.shape[1:]), lambda s: (v, 0, 0)) for n, m in enumerate(mats[:5])},
            grid=(1,),
            scratch=[
                pltpu.VMEM((NY * WORK, NX), F32),
                pltpu.VMEM((ZD * NY, NX), F32),
                pltpu.SemaphoreType.DMA,
                pltpu.VMEM((2, NY * SLOT, NX), F32),
                pltpu.SemaphoreType.DMA((2,)),
            ],
            flops=5 << 30,
            moved=4 * big,
        )
        return low, high

    far_rec = pltpu.with_memory_space_constraint(rec, pltpu.HBM)
    views = rec.shape[0]
    send, *kept = call(
        pack_kernel,
        (pack, last, far_est),
        ((GRID, views, YT, ZD, NX), (1, YT, ZD, NX), (1, YT, ZD, NX)),
        ins={2: ANY},
        out_specs=[ANY, ANY, ANY],
        scratch=[
            pltpu.VMEM((ZD * NY, NX), F32),
            pltpu.VMEM((NY * WORK, NX), F32),
            pltpu.SemaphoreType.DMA((STEPS,)),
            pltpu.SemaphoreType.DMA,
            pltpu.SemaphoreType.DMA((views,)),
        ],
        moved=2 * big,
        far=(0, 1, 2),
    )
    recv = exchange(send, "slab")
    places = [arriving] + [shifted(arriving, "view", hop, True) for hop in range(1, PLANES)]
    recv, *rest = lax.optimization_barrier((recv, *mats, *places))
    mats, places = rest[: len(mats)], rest[len(mats) :]
    parts0 = padded(*unpacked(0, recv, kept[0]))
    recv = after(recv, parts0[1])
    parts1 = padded(*unpacked(1, recv, kept[1]))
    back0 = blurred(0, parts0)
    ready0 = padded(*back0)
    parts1 = lax.optimization_barrier((*parts1, *back0))[:4]
    back1 = blurred(1, parts1)
    ready1 = padded(*back1)
    half = (GRID, views, 2, ZD, NX)

    def rows_of_tiles(at, which):
        return {at + n: pl.BlockSpec((GRID, 2, PAD, NX), lambda s: (0, which, 0, 0)) for n in range(4)}

    def adjoint_first(v, parts, buffer=None):
        operands = (chosen, *[p.reshape(GRID, YT, PAD, NX) for p in parts], mats[5])
        return call(
            functools.partial(adjoint_first_kernel, v),
            operands if buffer is None else (*operands, buffer),
            (half, (2, ZD, NX)),
            ins=rows_of_tiles(1, 0) | {6: ANY},
            out_specs=[
                pl.BlockSpec((GRID // 2, 1, 2, ZD, NX), lambda s: (s, v, 0, 0, 0)),
                pl.BlockSpec((2, ZD, NX), lambda s: (0, 0, 0)),
            ],
            grid=(2,),
            flops=1 << 30,
            moved=2 * big,
            far=(0,),
            alias={} if buffer is None else {6: 0},
        )

    def adjoint_last(v, parts):
        return call(
            functools.partial(adjoint_last_kernel, v),
            (chosen, plane.reshape(1), *[p.reshape(GRID, YT, PAD, NX) for p in parts], mats[5]),
            ((GRID + 1, PAD, NX),) * PLANES,
            ins=rows_of_tiles(2, 1),
            grid=(1,),
            scratch=[pltpu.VMEM((GRID + 1, 2 * ZD, NX), F32)],
            flops=1 << 30,
            moved=2 * big,
        )

    def across(parts):
        return [shifted(p, "view", hop, True) for hop, p in enumerate(parts) if hop]

    last0 = adjoint_last(0, ready0)
    last0 = [last0[0], *across(last0)]
    send, kept0 = adjoint_first(0, ready0)
    send, kept1 = adjoint_first(1, ready1, send)
    recv = exchange(send, "slab")
    last1 = adjoint_last(1, ready1)
    last1 = [last1[0], *across(last1)]
    send, kept = call(
        gather_kernel,
        [part for pair in zip(last0, last1) for part in pair],
        ((GRID, PLANES, views, PAD, NX), (PLANES, views, PAD, NX)),
        out_specs=[ANY, VMEM],
        scratch=[pltpu.SemaphoreType.DMA((PLANES * views,))],
        moved=2 * big,
        far=(0,),
    )
    recv1 = exchange(after(send, recv), "slab")
    block = (GRID // PLANES, 2, ZD, NX)
    products = call(
        product_first_kernel, (arriving, plane.reshape(1), recv, kept0, kept1), (block,) * PLANES, moved=2 * big
    )
    arrived = across(products)
    (mine,) = call(quarter_kernel, (products[0], *arrived), (block,), moved=big)
    pieces = [mine] + [shifted(mine, "view", hop, True) for hop in range(1, PLANES)]
    (product,) = call(product_last_kernel, (*places, recv1, kept), ((GRID, PAD, NX),), moved=2 * big)
    pieces += [product] + [shifted(product, "view", hop, True) for hop in range(1, PLANES)]
    where = (plane - jnp.arange(PLANES, dtype=jnp.int32)) % PLANES
    blocks = {1: pl.BlockSpec((ROWS * NY, NX), lambda s: (s, 0))}
    for n in range(PLANES):
        blocks[2 + n] = pl.BlockSpec((*block[:2], ROWS, NX), lambda s: (0, 0, s, 0))
    (out,) = call(
        final_kernel,
        (where, est, *pieces),
        ((ZD * NY, NX),),
        ins=blocks,
        out_specs=[pl.BlockSpec((ROWS * NY, NX), lambda s: (s, 0))],
        grid=(STEPS,),
        scratch=[pltpu.VMEM((ROWS * PITCH, NX), F32)],
        moved=3 * big,
    )
    return out.reshape(estimate.shape)


def solution(mesh):
    in_specs = (
        P("slab", None, None),
        P("view", "slab", None, None),
        P("view", None, None),
        P("view", None, None),
    )
    out_specs = P("slab", None, None)

    return jax.shard_map(local, mesh=mesh, in_specs=in_specs, out_specs=out_specs, check_vma=False)
```
